32 devices in a mesh: fsdp: 4 (over y, x), ctx: 4 (over z), tp: 2 (over core).
Axes of the slice: x: 2, y: 2, z: 4, core: 2. Of those that a mesh axis runs over, the one named last changes fastest.
Arguments:
- tokens: bfloat16 [2, 2048, 1536], P(None, ('fsdp', 'ctx')), may hold values from -6 to 6
- gain_attn: bfloat16 [1536], P('fsdp'), may hold values from 0.5 to 1.5
- w_query: bfloat16 [1536, 1536], P('fsdp', 'tp'), may hold values from -0.15625 to 0.15625
- key_projection_weight: bfloat16 [1536, 256], P('fsdp', 'tp'), may hold values from -0.15625 to 0.15625
- value_projection_weight: bfloat16 [1536, 256], P('fsdp', 'tp'), may hold values from -0.15625 to 0.15625
- w_output: bfloat16 [1536, 1536], P('tp', 'fsdp'), may hold values from -1.25 to 1.25
- gain_mlp: bfloat16 [1536], P('fsdp'), may hold values from 0.5 to 1.5
- w_router: bfloat16 [1536, 8], P('fsdp'), may hold values from -0.078125 to 0.078125
- w_gate: bfloat16 [8, 1536, 768], P(None, 'fsdp', 'tp'), may hold values from -0.15625 to 0.15625
- w_up: bfloat16 [8, 1536, 768], P(None, 'fsdp', 'tp'), may hold values from -0.15625 to 0.15625
- w_down: bfloat16 [8, 768, 1536], P(None, 'tp', 'fsdp'), may hold values from -0.875 to 0.875
- lineage: int32 [2, 3, 2048], replicated, may hold values from -1 to 13, as said below
- expert_ids: int32 [2, 2048, 4], P(None, ('fsdp', 'ctx')), may hold values from 0 to 7, all different within a row; in each aligned block of 128 rows (0 to 127, 128 to 255, ..., all dimensions but the last counted through in order) at most 96 rows name the same one
- cotangent: bfloat16 [2, 2048, 1536], P(None, ('fsdp', 'ctx')), may hold values from -6 to 6
Outputs:
- output: bfloat16 [2, 2048, 1536], P(None, ('fsdp', 'ctx'))
- input_grad: float32 [2, 2048, 1536], P(None, ('fsdp', 'ctx'))
- grad_gain_attn: float32 [1536], P('fsdp')
- grad_w_query: float32 [1536, 1536], P('fsdp', 'tp')
- grad_w_key: float32 [1536, 256], P('fsdp', 'tp')
- grad_w_value: float32 [1536, 256], P('fsdp', 'tp')
- grad_w_output: float32 [1536, 1536], P('tp', 'fsdp')
- grad_gain_mlp: float32 [1536], P('fsdp')
- grad_w_router: float32 [1536, 8], P('fsdp')
- grad_w_gate: float32 [8, 1536, 768], P(None, 'fsdp', 'tp')
- grad_w_up: float32 [8, 1536, 768], P(None, 'fsdp', 'tp')
- grad_w_down: float32 [8, 768, 1536], P(None, 'tp', 'fsdp')
The draws below stay inside these ranges and needn't reach their ends.
Inputs may be any that keep to these rules, and one draw needn't show every extreme that they name: `lineage`: in each micro-batch row 0 gives each slot's segment, rows 1 and 2 the segments of its parent and grandparent, -1 where there is none. Segments are contiguous runs of slots; a parent's slots precede its children's. A micro-batch holds a tree of a trunk, four branches and two leaves on each branch, and a tree that is only a trunk. `expert_ids`: among the 128 tokens of one device (aligned blocks of the slots of a micro-batch), no expert is named by more than 96 tokens, a bound that some block reaches.
All inputs are finite; a program needn't handle non-finite values.
Results may differ from the reference program's by a relative error of at most 0.024.
Values may be sent and summed in bfloat16 or wider, within the bound.
No kernel may reach another device: no remote copies, remote signals or barrier semaphores. Data moves between devices by JAX's collectives and lax.ppermute only.
A program may use at most 136 MiB of HBM per device.

```python
import math
import jax
import jax.numpy as jnp
import numpy as np
from jax import lax

MODEL_WIDTH = 1536
QUERY_HEADS = 12
KEY_VALUE_HEADS = 2
HEAD_SIZE = 128
FF = 768
TOPK = 4
EXPERTS = 8
MICRO = 2
TOK_DEV = 128
MB_TOK = 2048
UNIT = 64
CAP = 96


def one_tree(key):
    extra_key, place_key = jax.random.split(key)
    shuffled = jax.random.permutation(extra_key, 10)
    extra_units = jnp.concatenate([jnp.array([0, 0, 1, 1], jnp.int32), (shuffled < 2).astype(jnp.int32)])
    segment = jnp.arange(14, dtype=jnp.int32)
    length = jnp.where(segment < 2, 8 * UNIT, UNIT * (1 + extra_units))
    solo_place = jax.random.randint(place_key, (), 0, 4)
    branch_num = (segment - 2) // 3
    within = (segment - 2) % 3
    sort_key = jnp.where(segment == 0, 0, jnp.where(segment == 1, 10 * (1 + solo_place) - 5, 10 * (1 + branch_num) + within))
    seg_start = jnp.sum(jnp.where(sort_key[None, :] < sort_key[:, None], length[None, :], 0), 1)
    parent = jnp.where(segment < 2, -1, jnp.where(within == 0, 0, 2 + 3 * branch_num))
    grand_parent = jnp.where((segment >= 2) & (within > 0), 0, -1)
    slot_index = jnp.arange(MB_TOK, dtype=jnp.int32)
    inside = ((slot_index[None, :] >= seg_start[:, None]) & (slot_index[None, :] < (seg_start + length)[:, None])).astype(jnp.int32)
    own_seg = jnp.sum(segment[:, None] * inside, 0)
    parent_of = jnp.sum(parent[:, None] * inside, 0)
    grand_of = jnp.sum(grand_parent[:, None] * inside, 0)
    return jnp.stack([own_seg, parent_of, grand_of]).astype(jnp.int32)


def draw_lineage(key, part):
    return jax.vmap(one_tree)(jax.random.split(key, MICRO))


def shard_levels(rng, extent, cuts, smallest, high):
    loudness = 1.0
    for dim, parts in cuts:
        draws = jax.random.uniform(jax.random.fold_in(jax.random.fold_in(rng, 6), dim), (parts,), jnp.float32, smallest / len(cuts), high / len(cuts))
        loudness = loudness * jnp.repeat(jnp.exp(draws), extent[dim] // parts).reshape((-1,) + (1,) * (len(extent) - 1 - dim))
    return loudness


def routed_block(key, own, number, rows, amount, top, reach, skew):
    ranking = jax.random.permutation(key, amount)
    packed, ordinary = portions_of(amount, rows * top, reach, skew, True), portions_of(amount, rows * top, reach, skew, False)
    places = jnp.arange(amount)

    def named(lengths, turn):
        used = int((lengths > 0).sum())
        fixed = max(1, used // 4)
        shifted = fixed + (places - fixed + turn * (used - fixed)) % max(1, amount - fixed)
        return jnp.zeros((amount,), jnp.int32).at[ranking[jnp.where(places < fixed, places, shifted)]].set(jnp.asarray(lengths, jnp.int32))

    lengths = jnp.where(number % 4 == 0, named(packed, number // 4), named(ordinary, number - number // 4 - 1))
    mixed = jax.random.permutation(jax.random.fold_in(own, 3), amount)
    source_of, taker = mixed[0:amount // 2 * 2:2], mixed[1:amount // 2 * 2:2]
    margin = jnp.minimum(lengths[source_of] - 1, reach - lengths[taker]) // 2
    margin = jnp.where((source_of == ranking[0]) | (taker == ranking[0]) | (lengths[taker] == 0), 0, jnp.maximum(margin, 0))
    shifted = jax.random.randint(jax.random.fold_in(own, 4), (amount // 2,), 0, 1 << 20) % (margin + 1)
    lengths = lengths.at[source_of].add(-shifted).at[taker].add(shifted)
    members = jnp.searchsorted(jnp.cumsum(lengths), jnp.arange(rows * top), side="right").astype(jnp.int32)
    table = members.reshape(top, rows).T
    table = table[jax.random.permutation(jax.random.fold_in(own, 1), rows)]
    turn = jax.random.randint(jax.random.fold_in(own, 2), (rows, 1), 0, top)
    return jnp.take_along_axis(table, (jnp.arange(top)[None, :] + turn) % top, axis=1)


def portions_of(number_of, total, reach, lean, full):
    loads = [(1 << 20) // math.isqrt(grade ** lean) + 1 for grade in range(1, number_of + 1)]
    largest = reach if full else min(reach, max(-(-total // number_of), total * loads[0] // sum(loads)))
    least = 1 if total - largest >= number_of - 1 else 0
    given, surplus = [largest] + [least] * (number_of - 1), total - largest - least * (number_of - 1)
    while surplus > 0:
        movable = [i for i in range(1, number_of) if given[i] < largest] or [i for i in range(1, number_of) if given[i] < reach]
        mass, remaining = sum([loads[i] for i in movable]), surplus
        for i in movable:
            extra = min(reach - given[i], max(1, remaining * loads[i] // mass), surplus)
            given[i] = given[i] + extra
            surplus = surplus - extra
    return np.array(given)


def centred(rng, shape, deviation, bound, cuts=(), kind=jnp.bfloat16):
    values = jax.random.normal(rng, shape, jnp.float32) * deviation
    if len(cuts) > 0:
        values = shard_levels(rng, shape, cuts, -0.22, 0.18) * values
    return jnp.clip(values, min=-bound, max=bound).astype(kind)


def setup_inputs(seed: int = 0) -> dict:
    splits = jax.random.split(jax.random.key(seed), 15)
    tokens = centred(splits[0], (MICRO, MB_TOK, MODEL_WIDTH), 1.0, 6.0, ((1, 16),))
    gain_attn = jnp.clip(1.0 + 0.1 * jax.random.normal(splits[1], (MODEL_WIDTH,), jnp.float32), 0.5, 1.5).astype(jnp.bfloat16)
    w_query = centred(splits[2], (MODEL_WIDTH, QUERY_HEADS * HEAD_SIZE), MODEL_WIDTH ** -0.5, 0.15625, ((0, 4), (1, 2)))
    key_projection_weight = centred(splits[3], (MODEL_WIDTH, KEY_VALUE_HEADS * HEAD_SIZE), MODEL_WIDTH ** -0.5, 0.15625, ((0, 4), (1, 2)))
    value_projection_weight = centred(splits[4], (MODEL_WIDTH, KEY_VALUE_HEADS * HEAD_SIZE), MODEL_WIDTH ** -0.5, 0.15625, ((0, 4), (1, 2)))
    w_output = centred(splits[5], (QUERY_HEADS * HEAD_SIZE, MODEL_WIDTH), (max(1, QUERY_HEADS * HEAD_SIZE * 32 // MB_TOK)) ** -0.5, 1.25, ((0, 2), (1, 4)))
    gain_mlp = jnp.clip(1.0 + 0.1 * jax.random.normal(splits[6], (MODEL_WIDTH,), jnp.float32), 0.5, 1.5).astype(jnp.bfloat16)
    w_router = centred(splits[7], (MODEL_WIDTH, EXPERTS), (4 * MODEL_WIDTH) ** -0.5, 0.078125, ((0, 4),))
    w_gate = centred(splits[8], (EXPERTS, MODEL_WIDTH, FF), MODEL_WIDTH ** -0.5, 0.15625, ((1, 4), (2, 2)))
    w_up = centred(splits[9], (EXPERTS, MODEL_WIDTH, FF), MODEL_WIDTH ** -0.5, 0.15625, ((1, 4), (2, 2)))
    w_down = centred(splits[10], (EXPERTS, FF, MODEL_WIDTH), (FF // 16) ** -0.5, 0.875, ((1, 2), (2, 4)))
    lineage = draw_lineage(jax.random.fold_in(splits[14], 71), 0)
    expert_ids_keys = jax.random.split(jax.random.fold_in(splits[12], 1), MICRO * MB_TOK // TOK_DEV)
    expert_ids_turns = jax.random.permutation(jax.random.fold_in(splits[12], 3), MICRO * MB_TOK // TOK_DEV)
    expert_ids = jax.vmap(lambda own, number: routed_block(jax.random.fold_in(splits[12], 2), own, number, TOK_DEV, EXPERTS, TOPK, CAP, 1))(expert_ids_keys, expert_ids_turns).reshape((MICRO, MB_TOK, TOPK))
    cotangent = centred(splits[13], (MICRO, MB_TOK, MODEL_WIDTH), 1.0, 6.0, ((1, 16),))
    return dict(tokens=tokens, gain_attn=gain_attn, w_query=w_query, key_projection_weight=key_projection_weight, value_projection_weight=value_projection_weight, w_output=w_output, gain_mlp=gain_mlp, w_router=w_router, w_gate=w_gate, w_up=w_up, w_down=w_down, lineage=lineage, expert_ids=expert_ids, cotangent=cotangent)


EPSILON = 1e-06
ROPE_BASE = 1000000.0
NEG_FILL = -1e+30

@jax.custom_vjp
def reduced_precision(v):
    return lax.optimization_barrier(v.astype(jnp.bfloat16)).astype(jnp.float32)

@jax.custom_vjp
def reduced_precision_backward(v):
    return v

def low_keep(v):
    return (reduced_precision(v), None)

def low_pass(kept, grad):
    return (grad,)

def back_keep(v):
    return (v, None)

def back_low(kept, grad):
    return (reduced_precision(grad),)
reduced_precision.defvjp(low_keep, low_pass)
reduced_precision_backward.defvjp(back_keep, back_low)

def normed(values, gain):
    return values * lax.rsqrt(lax.optimization_barrier(jnp.mean(values * values, -1, keepdims=True)) + EPSILON) * gain

def rotary_embedding(values, tree_positions):
    half_dim = values.shape[-1] // 2
    frequency = ROPE_BASE ** (-jnp.arange(half_dim, dtype=jnp.float32) / half_dim)
    angles = tree_positions[:, None] * frequency[None, :]
    cosine = jnp.cos(angles)[:, None, :]
    sine_val = jnp.sin(angles)[:, None, :]
    first_half = values[..., :half_dim]
    second_half = values[..., half_dim:]
    return jnp.concatenate([first_half * cosine - second_half * sine_val, second_half * cosine + first_half * sine_val], -1)

def allowed(query_lin, query_index, key_owner, key_index):
    same_seg = (key_owner[None, :] == query_lin[0][:, None]) & (key_index[None, :] <= query_index[:, None])
    return same_seg | (key_owner[None, :] == query_lin[1][:, None]) | (key_owner[None, :] == query_lin[2][:, None])

def path_places(lineage_mb, rows_per_block):
    expert_slot_total = lineage_mb.shape[1]
    key_index = jnp.arange(expert_slot_total, dtype=jnp.int32)

    def count_block(first_row_offset):
        query_lin = lax.dynamic_slice_in_dim(lineage_mb, first_row_offset, rows_per_block, 1)
        query_index = first_row_offset + jnp.arange(rows_per_block, dtype=jnp.int32)
        return lax.optimization_barrier(jnp.sum(allowed(query_lin, query_index, lineage_mb[0], key_index).astype(jnp.int32), -1)) - 1
    starts = jnp.arange(expert_slot_total // rows_per_block, dtype=jnp.int32) * rows_per_block
    return lax.map(count_block, starts).reshape(expert_slot_total)

def layer_forward(lineage_mb, route_ids, rows_per_block, tokens_in, gain_attn, w_query, key_projection_weight, value_projection_weight, w_output, gain_mlp, w_router, w_gate, w_up, w_down):
    exact_precision = lax.Precision.HIGHEST
    expert_slot_total = tokens_in.shape[0]
    tree_positions = path_places(lineage_mb, rows_per_block).astype(jnp.float32)
    normalized_input = reduced_precision(normed(tokens_in, gain_attn))
    query_pre = reduced_precision_backward(jnp.dot(normalized_input, w_query, precision=exact_precision))
    key_before_rotation = reduced_precision_backward(jnp.dot(normalized_input, key_projection_weight, precision=exact_precision))
    value_rows_full = reduced_precision(reduced_precision_backward(jnp.dot(normalized_input, value_projection_weight, precision=exact_precision))).reshape(expert_slot_total, KEY_VALUE_HEADS, HEAD_SIZE)
    query_rows = reduced_precision(rotary_embedding(query_pre.reshape(expert_slot_total, QUERY_HEADS, HEAD_SIZE), tree_positions))
    key_rows = reduced_precision(rotary_embedding(key_before_rotation.reshape(expert_slot_total, KEY_VALUE_HEADS, HEAD_SIZE), tree_positions))
    query_group_width = QUERY_HEADS // KEY_VALUE_HEADS
    scale_factor = HEAD_SIZE ** (-0.5)
    key_index = jnp.arange(expert_slot_total, dtype=jnp.int32)

    def attend(first_row_offset):
        query_tile = lax.dynamic_slice_in_dim(query_rows, first_row_offset, rows_per_block, 0).reshape(rows_per_block, KEY_VALUE_HEADS, query_group_width, HEAD_SIZE)
        scores = reduced_precision_backward(jnp.einsum('qhgd,khd->qhgk', query_tile, key_rows, precision=exact_precision) * scale_factor)
        query_lin = lax.dynamic_slice_in_dim(lineage_mb, first_row_offset, rows_per_block, 1)
        query_index = first_row_offset + jnp.arange(rows_per_block, dtype=jnp.int32)
        visible = allowed(query_lin, query_index, lineage_mb[0], key_index)
        scores = jnp.where(visible[:, None, None, :], scores, NEG_FILL)
        row_max = lax.optimization_barrier(jnp.max(scores, -1, keepdims=True))
        exp_scores = jnp.exp(scores - row_max)
        soft_probs = reduced_precision(exp_scores / lax.optimization_barrier(jnp.sum(exp_scores, -1, keepdims=True)))
        return jnp.einsum('qhgk,khd->qhgd', soft_probs, value_rows_full, precision=exact_precision).reshape(rows_per_block, QUERY_HEADS * HEAD_SIZE)
    starts = jnp.arange(expert_slot_total // rows_per_block, dtype=jnp.int32) * rows_per_block
    attended = lax.map(jax.checkpoint(attend), starts).reshape(expert_slot_total, QUERY_HEADS * HEAD_SIZE)
    attended = reduced_precision(reduced_precision_backward(attended))
    branch = reduced_precision_backward(jnp.dot(attended, w_output, precision=exact_precision))
    middle = tokens_in + branch
    mixed_in = reduced_precision(normed(middle, gain_mlp))
    logits = jnp.dot(mixed_in, w_router, precision=exact_precision)
    router_exp = jnp.exp(logits - lax.optimization_barrier(jnp.max(logits, -1, keepdims=True)))
    router_probs = router_exp / lax.optimization_barrier(jnp.sum(router_exp, -1, keepdims=True))
    chosen = lax.optimization_barrier(jnp.sum((route_ids[:, :, None] == jnp.arange(EXPERTS, dtype=jnp.int32)[None, None, :]).astype(jnp.float32), 1))
    combine = router_probs * chosen

    def expert_step(carried, pieces):
        gate_mat, up_mat, down_mat, weight_col = pieces
        gate_val = reduced_precision_backward(jnp.dot(mixed_in, gate_mat, precision=exact_precision))
        up_val = reduced_precision_backward(jnp.dot(mixed_in, up_mat, precision=exact_precision))
        hidden = reduced_precision(jax.nn.gelu(gate_val) * up_val)
        expert_out = reduced_precision_backward(jnp.dot(hidden, down_mat, precision=exact_precision))
        return (carried + weight_col[:, None] * expert_out, None)
    summed, unused = lax.scan(jax.checkpoint(expert_step), jnp.zeros_like(middle), (w_gate, w_up, w_down, combine.T))
    return middle + summed

def reference(tokens, gain_attn, w_query, key_projection_weight, value_projection_weight, w_output, gain_mlp, w_router, w_gate, w_up, w_down, lineage, expert_ids, cotangent):
    weights = tuple((array.astype(jnp.float32) for array in (gain_attn, w_query, key_projection_weight, value_projection_weight, w_output, gain_mlp, w_router, w_gate, w_up, w_down)))
    rows_per_block = math.gcd(MB_TOK, 512)
    outputs = []
    input_grads = []
    totals = tuple((jnp.zeros_like(array) for array in weights))
    for batch_index in range(MICRO):
        lineage_mb = lineage[batch_index]
        route_ids = expert_ids[batch_index]

        def forward(tokens_in, gain_one, query_mat, key_mat, value_mat, output_mat, gain_two, router_mat, gate_mats, up_mats, down_mats):
            return layer_forward(lineage_mb, route_ids, rows_per_block, tokens_in, gain_one, query_mat, key_mat, value_mat, output_mat, gain_two, router_mat, gate_mats, up_mats, down_mats)
        result, pullback = jax.vjp(forward, tokens[batch_index].astype(jnp.float32), weights[0], weights[1], weights[2], weights[3], weights[4], weights[5], weights[6], weights[7], weights[8], weights[9])
        grad_list = pullback(cotangent[batch_index].astype(jnp.float32))
        outputs.append(result.astype(jnp.bfloat16))
        input_grads.append(grad_list[0])
        totals = tuple((running + grad_piece for running, grad_piece in zip(totals, grad_list[1:])))
    return (jnp.stack(outputs), jnp.stack(input_grads), totals[0], totals[1], totals[2], totals[3], totals[4], totals[5], totals[6], totals[7], totals[8], totals[9])
```

```python
import jax
import jax.numpy as jnp
from jax import lax
from jax.experimental import pallas as pl
from jax.experimental.pallas import tpu as pltpu
from jax.sharding import PartitionSpec as P

HEAD = 128
LANES = 128
EPSILON = 1e-06
ROPE_BASE = 1000000.0
NEG_FILL = -1e30
KEY_STEP = 256
MOE_ROWS = 512
VMEM_BYTES = 60 * 2**20

f32 = jnp.float32
bf16 = jnp.bfloat16
EXACT = lax.Precision.HIGHEST
NN = (((1,), (0,)), ((), ()))
NT = (((1,), (1,)), ((), ()))
TN = (((0,), (0,)), ((), ()))


def mm(left, right, dims=NN, precision=None):
    return lax.dot_general(left, right, dims, precision=precision, preferred_element_type=f32)


def vmem(count):
    return [pl.BlockSpec(memory_space=pltpu.VMEM)] * count


def anywhere(count):
    return [pl.BlockSpec(memory_space=pl.ANY)] * count


def scalars():
    return [pl.BlockSpec(memory_space=pltpu.SMEM)]


def shape(dims, kind):
    return jax.ShapeDtypeStruct(dims, kind)


def cost(flops, moved):
    return pl.CostEstimate(flops=int(flops), bytes_accessed=int(moved), transcendentals=0)


def params():
    return pltpu.CompilerParams(vmem_limit_bytes=VMEM_BYTES)


def swap(value, axis, size, bit):
    return lax.ppermute(value, axis, [(i, i ^ bit) for i in range(size)])


def low_bit(number):
    return number & -number


def high_bit(number):
    return 1 << (number.bit_length() - 1)


def gather_relative(own, axis, size, high):
    pick = high_bit if high else low_bit
    got = [own] + [None] * (size - 1)
    for j in range(1, size):
        bit = pick(j)
        got[j] = swap(got[j ^ bit], axis, size, bit)
    return got


def add_low(left, right):
    return (left.astype(f32) + right.astype(f32)).astype(bf16)


def scatter_relative(blocks, axis, size, high):
    current = dict(enumerate(blocks))
    bits = [1 << k for k in range(size.bit_length() - 1)]
    for bit in reversed(bits) if high else bits:
        current = {
            j: add_low(current[j], swap(current[j | bit], axis, size, bit))
            for j in current
            if not j & bit
        }
    return current[0]


def exchange_direct(blocks, axis, size):
    return [blocks[0]] + [swap(blocks[j], axis, size, j) for j in range(1, size)]


def ordered(blocks, index):
    count = len(blocks)
    bit = 1
    while bit < count:
        flag = (index & bit) != 0
        blocks = [jnp.where(flag, blocks[i ^ bit], blocks[i]) for i in range(count)]
        bit *= 2
    return blocks


def axis_relative(value, dim, index):
    count, bit, dims = value.shape[dim], 1, value.shape
    while bit < count:
        split = value.reshape(*dims[:dim], count // (2 * bit), 2, bit, *dims[dim + 1 :])
        value = jnp.where((index & bit) != 0, jnp.flip(split, dim + 1), split).reshape(dims)
        bit *= 2
    return value


def lanes_relative(value, index, count):
    width = value.shape[-1] // count
    return jnp.concatenate(
        [
            lax.dynamic_slice_in_dim(value, (index ^ j) * width, width, value.ndim - 1)
            for j in range(count)
        ],
        -1,
    )


def rotated(values, cosine, sine):
    return values * cosine + pltpu.roll(values, HEAD // 2, 1) * sine


def norm_scale(values):
    return lax.rsqrt(jnp.mean(values * values, -1, keepdims=True) + EPSILON)


def fetch(sources, targets, sems):
    copies = [
        pltpu.make_async_copy(source, target, sems.at[number])
        for number, (source, target) in enumerate(zip(sources, targets))
    ]
    for copy in copies:
        copy.start()
    return copies


def project_in(x, gain, cosine, sine, weights, micro, rows):
    total, width = x.shape
    parts = len(weights)
    depth, half = weights[0].shape
    heads = (2 * half - 2 * HEAD) // HEAD

    def body(x_ref, gain_ref, cos_ref, sin_ref, *rest):
        w_refs, (a_ref, q_ref, kv_ref, all_ref, sems) = rest[:parts], rest[parts:]
        copies = fetch(
            w_refs,
            [
                all_ref.at[pl.ds(n // 2 * depth, depth), pl.ds(n % 2 * half, half)]
                for n in range(parts)
            ],
            sems,
        )
        values = x_ref[...].astype(f32)
        a_ref[...] = (values * norm_scale(values) * gain_ref[...]).astype(bf16)
        for copy in copies:
            copy.wait()
        for m in range(micro):
            span = slice(m * rows, (m + 1) * rows)
            mixed = mm(a_ref[span, :], all_ref[...])
            cosine_m, sine_m = cos_ref[span, :], sin_ref[span, :]
            for h in range(heads):
                q_ref[m, h * rows : (h + 1) * rows, :] = rotated(
                    mixed[:, h * HEAD : (h + 1) * HEAD], cosine_m, sine_m
                ).astype(bf16)
            kv_ref[m, :, :HEAD] = rotated(
                mixed[:, heads * HEAD : (heads + 1) * HEAD], cosine_m, sine_m
            ).astype(bf16)
            kv_ref[m, :, HEAD:] = mixed[:, (heads + 1) * HEAD :].astype(bf16)

    return pl.pallas_call(
        body,
        name="project_in",
        out_shape=(
            shape((total, width), bf16),
            shape((micro, heads * rows, HEAD), bf16),
            shape((micro, rows, 2 * HEAD), bf16),
            shape((width, 2 * half), bf16),
        ),
        in_specs=vmem(4) + anywhere(parts),
        out_specs=tuple(vmem(4)),
        scratch_shapes=[pltpu.SemaphoreType.DMA((parts,))],
        compiler_params=params(),
        cost_estimate=cost(2 * total * width * 2 * half, 2 * 2 * width * 2 * half),
    )(x, gain, cosine, sine, *weights)


def attend(seen, q, mask, kv, weights):
    micro, stacked, _ = q.shape
    keys, rows = mask.shape[1], mask.shape[2]
    heads = stacked // rows
    blocks, parts = len(kv), len(weights)
    per_block = keys // blocks
    depth, half = weights[0].shape
    width = depth * parts // 2
    steps = keys // KEY_STEP
    scale = HEAD ** (-0.5)

    def body(seen_ref, q_ref, mask_ref, *rest):
        kv_refs, w_refs = rest[:blocks], rest[blocks : blocks + parts]
        branch_ref, o_ref, lse_ref, wo_ref, kv_all, top, total, acc, kv_sems, w_sems = rest[
            blocks + parts :
        ]
        kv_copies = fetch(
            kv_refs, [kv_all.at[:, pl.ds(j * per_block, per_block), :] for j in range(blocks)], kv_sems
        )
        w_copies = fetch(
            w_refs,
            [
                wo_ref.at[pl.ds(n // 2 * depth, depth), pl.ds(n % 2 * half, half)]
                for n in range(parts)
            ],
            w_sems,
        )
        for copy in kv_copies:
            copy.wait()
        for m in range(micro):
            top[...] = jnp.full_like(top, NEG_FILL)
            total[...] = jnp.zeros_like(total)
            acc[...] = jnp.zeros_like(acc)
            queries = q_ref[m]

            def step(n, carry, m=m, queries=queries):
                @pl.when(seen_ref[m * steps + n] > 0)
                def _():
                    start = pl.multiple_of(n * KEY_STEP, KEY_STEP)
                    keys_n = kv_all[m, pl.ds(start, KEY_STEP), :HEAD]
                    values_n = kv_all[m, pl.ds(start, KEY_STEP), HEAD:]
                    bias = mask_ref[m, pl.ds(start, KEY_STEP), :].astype(f32)
                    scores = mm(keys_n, queries, NT) * scale + jnp.concatenate([bias] * heads, 1)
                    peak = jnp.maximum(top[...], jnp.max(scores, 0, keepdims=True))
                    rescale = jnp.exp(top[...] - peak)
                    weights_n = jnp.exp(scores - peak)
                    total[...] = total[...] * rescale + jnp.sum(weights_n, 0, keepdims=True)
                    acc[...] = acc[...] * rescale + mm(values_n, weights_n.astype(bf16), TN)
                    top[...] = peak

                return carry

            lax.fori_loop(0, steps, step, 0)
            lse_ref[m] = top[...] + jnp.log(total[...])
            mixed = acc[...] / total[...]
            for h in range(heads):
                o_ref[m, :, h * HEAD : (h + 1) * HEAD] = mixed[
                    :, h * rows : (h + 1) * rows
                ].T.astype(bf16)
        for copy in w_copies:
            copy.wait()
        for m in range(micro):
            branch_ref[m] = mm(o_ref[m], wo_ref[...], NT).astype(bf16)

    return pl.pallas_call(
        body,
        name="attend",
        out_shape=(
            shape((micro, rows, width), bf16),
            shape((micro, rows, heads * HEAD), bf16),
            shape((micro, 1, stacked), f32),
            shape((width, heads * HEAD), bf16),
        ),
        in_specs=scalars() + vmem(2) + anywhere(blocks + parts),
        out_specs=tuple(vmem(4)),
        scratch_shapes=[
            pltpu.VMEM((micro, keys, 2 * HEAD), bf16),
            pltpu.VMEM((1, stacked), f32),
            pltpu.VMEM((1, stacked), f32),
            pltpu.VMEM((HEAD, stacked), f32),
            pltpu.SemaphoreType.DMA((blocks,)),
            pltpu.SemaphoreType.DMA((parts,)),
        ],
        compiler_params=params(),
        cost_estimate=cost(
            2 * micro * stacked * keys * HEAD * 2 + 2 * micro * rows * width * heads * HEAD,
            2 * micro * keys * 2 * HEAD + 2 * width * heads * HEAD * 2,
        ),
    )(seen, q, mask, *kv, *weights)


def second_norm(place, x, branch, other, gain):
    rows, width = other.shape

    def body(place_ref, x_ref, branch_ref, other_ref, gain_ref, middle_ref, b_ref):
        t = place_ref[2]
        middle = (
            x_ref[t].astype(f32) + branch_ref[t].astype(f32) + other_ref[...].astype(f32)
        )
        middle_ref[...] = middle
        b_ref[...] = (middle * norm_scale(middle) * gain_ref[...]).astype(bf16)

    return pl.pallas_call(
        body,
        name="second_norm",
        out_shape=(shape((rows, width), f32), shape((rows, width), bf16)),
        in_specs=scalars() + vmem(4),
        out_specs=tuple(vmem(2)),
        compiler_params=params(),
        cost_estimate=cost(10 * rows * width, 20 * rows * width),
    )(place, x, branch, other, gain)


def routing(b, router, experts):
    logits = mm(b, router)
    lane = lax.broadcasted_iota(jnp.int32, logits.shape, 1)
    logits = jnp.where(lane < experts, logits, NEG_FILL)
    powers = jnp.exp(logits - jnp.max(logits, -1, keepdims=True))
    return powers / jnp.sum(powers, -1, keepdims=True), lane


def experts_step(place, b, cx, router, weights, experts):
    chunks, rows, width = b.shape
    local = len(weights)
    parts = len(weights[0])
    _, depth, hidden = weights[0][0].shape
    k0 = 0.7978845608028654
    k1 = 0.044715

    def body(place_ref, b_ref, cx_ref, router_ref, *rest):
        w_refs = rest[: local * parts]
        rest = rest[local * parts :]
        out_ref, back_ref = rest[:2]
        grad_refs = rest[2 : 2 + local * parts]
        w_all, b_turned, c_turned, gate_all, out_acc, back_acc, share_acc, grad_acc, stage, w_sems, g_sems = rest[
            2 + local * parts :
        ]
        chunk, e = pl.program_id(0), pl.program_id(1)

        def weight_copies(number):
            return [
                pltpu.make_async_copy(
                    w_refs[number * parts + j],
                    w_all.at[number, :, pl.ds(j * depth, depth), :],
                    w_sems.at[number * parts + j],
                )
                for j in range(parts)
            ]

        def grad_copies(number):
            return [
                pltpu.make_async_copy(
                    stage.at[:, pl.ds(j * depth, depth), :],
                    grad_refs[number * parts + j],
                    g_sems.at[number * parts + j],
                )
                for j in range(parts)
            ]

        @pl.when((chunk == 0) & (e == 0))
        def _():
            for number in range(local):
                for copy in weight_copies(number):
                    copy.start()

        @pl.when(e == 0)
        def _():
            probs, _ = routing(b_ref[0], router_ref[...], experts)
            gate_all[...] = probs * cx_ref[0, :, width:].astype(f32)
            b_turned[...] = b_ref[0].T
            c_turned[...] = cx_ref[0, :, :width].T

        for number in range(local):

            @pl.when((chunk == 0) & (e == number))
            def _(number=number):
                for copy in weight_copies(number):
                    copy.wait()

        b_rows = b_ref[0]
        c_rows = cx_ref[0, :, :width]
        w_gate, w_up, w_down = w_all[e, 0], w_all[e, 1], w_all[e, 2]
        lane = lax.broadcasted_iota(jnp.int32, (rows, LANES), 1)
        mine = lane == place_ref[1] * local + e
        gate = jnp.sum(jnp.where(mine, gate_all[...], 0.0), -1, keepdims=True)
        z = mm(b_rows, w_gate)
        up = mm(b_rows, w_up)
        down_back = mm(c_rows, w_down)
        square = z * z
        bend = jnp.tanh(k0 * z * (1.0 + k1 * square))
        half = 0.5 * (1.0 + bend)
        active = z * half
        slope = half + 0.5 * z * (1.0 - bend * bend) * (k0 * (1.0 + 3.0 * k1 * square))
        hidden_rows = active * up
        share = jnp.sum(hidden_rows * down_back, -1, keepdims=True)
        scaled = (gate * hidden_rows).astype(bf16)
        hidden_back = gate * down_back
        gate_back = (hidden_back * up * slope).astype(bf16)
        up_back = (hidden_back * active).astype(bf16)
        def sum_up(acc, new):
            @pl.when(e == 0)
            def _():
                acc[...] = new

            @pl.when(e > 0)
            def _():
                acc[...] += new

        sum_up(share_acc, jnp.where(mine, share, 0.0))
        sum_up(out_acc, mm(scaled, w_down, NT))
        sum_up(back_acc, mm(gate_back, w_gate, NT) + mm(up_back, w_up, NT))

        @pl.when(e == local - 1)
        def _():
            out_ref[0] = out_acc[...].astype(bf16)
            back_ref[0, :, :width] = back_acc[...].astype(bf16)
            back_ref[0, :, width:] = share_acc[...].astype(bf16)

        for number in range(1, local):

            @pl.when((chunk == chunks - 1) & (e == number))
            def _(number=number):
                for copy in grad_copies(number - 1):
                    copy.wait()

        for n, (turned, back) in enumerate(
            ((b_turned, gate_back), (b_turned, up_back), (c_turned, scaled))
        ):
            new = mm(turned[...], back)

            @pl.when(chunk == 0)
            def _(n=n, new=new):
                grad_acc[e, n] = new

            @pl.when((chunk > 0) & (chunk < chunks - 1))
            def _(n=n, new=new):
                grad_acc[e, n] += new

            @pl.when(chunk == chunks - 1)
            def _(n=n, new=new):
                stage[n] = (grad_acc[e, n] + new).astype(bf16)

        for number in range(local):

            @pl.when((chunk == chunks - 1) & (e == number))
            def _(number=number):
                for copy in grad_copies(number):
                    copy.start()
                if number == local - 1:
                    for copy in grad_copies(number):
                        copy.wait()

    block = lambda lanes: pl.BlockSpec((1, rows, lanes), lambda i, j: (i, 0, 0))
    return pl.pallas_call(
        body,
        name="experts_step",
        grid=(chunks, local),
        out_shape=(
            shape((chunks, rows, width), bf16),
            shape((chunks, rows, width + LANES), bf16),
            *[shape((3, depth, hidden), bf16)] * (local * parts),
        ),
        in_specs=scalars()
        + [
            block(width),
            block(width + LANES),
            pl.BlockSpec((width, LANES), lambda i, j: (0, 0), pipeline_mode=pl.Buffered(1)),
        ]
        + anywhere(local * parts),
        out_specs=(block(width), block(width + LANES), *anywhere(local * parts)),
        scratch_shapes=[
            pltpu.VMEM((local, 3, width, hidden), bf16),
            pltpu.VMEM((width, rows), bf16),
            pltpu.VMEM((width, rows), bf16),
            pltpu.VMEM((rows, LANES), f32),
            pltpu.VMEM((rows, width), f32),
            pltpu.VMEM((rows, width), f32),
            pltpu.VMEM((rows, LANES), f32),
            pltpu.VMEM((local, 3, width, hidden), f32),
            pltpu.VMEM((3, width, hidden), bf16),
            pltpu.SemaphoreType.DMA((local * parts,)),
            pltpu.SemaphoreType.DMA((local * parts,)),
        ],
        compiler_params=params(),
        cost_estimate=cost(
            18 * chunks * rows * width * hidden * local,
            2 * (4 * chunks * rows * width + 6 * local * width * hidden),
        ),
    )(place, b, cx, router, *[block_j for one in weights for block_j in one])


def second_norm_back(sums, middle, b, cx, gain, router, experts):
    rows, width = middle.shape
    count = len(sums)

    def body(*refs):
        middle_ref, b_ref, cx_ref, gain_ref, router_ref = refs[count : count + 5]
        dmiddle_ref, go_ref, small_ref = refs[count + 5 :]
        total = refs[0][...].astype(f32)
        for ref in refs[1:count]:
            total += ref[...].astype(f32)
        share = total[:, width:] * cx_ref[:, width:].astype(f32)
        probs, lane = routing(b_ref[...], router_ref[...], experts)
        dl = probs * (share - jnp.sum(probs * share, -1, keepdims=True))
        db = total[:, :width] + mm(dl, router_ref[...].astype(f32), NT, EXACT)
        values = middle_ref[...]
        scale = norm_scale(values)
        normal = values * scale
        dn = db * gain_ref[...]
        dmiddle = cx_ref[:, :width].astype(f32) + scale * (
            dn - normal * jnp.mean(dn * normal, -1, keepdims=True)
        )
        dmiddle_ref[...] = dmiddle
        go_ref[...] = dmiddle.astype(bf16)
        small_ref[...] = mm(b_ref[...].astype(f32), dl, TN, EXACT) + mm(
            db * normal, (lane == experts).astype(f32), TN, EXACT
        )

    return pl.pallas_call(
        body,
        name="second_norm_back",
        out_shape=(
            shape((rows, width), f32),
            shape((rows, width), bf16),
            shape((width, LANES), f32),
        ),
        in_specs=vmem(count + 5),
        out_specs=tuple(vmem(3)),
        compiler_params=params(),
        cost_estimate=cost(2 * 20 * rows * width * LANES, 24 * rows * width),
    )(*sums, middle, b, cx, gain, router)


def attend_back(place, seen, go_own, go_other, q, o, lse, mask, cosine, sine, wo, kv):
    micro, stacked, _ = q.shape
    keys, rows = mask.shape[1], mask.shape[2]
    heads = stacked // rows
    blocks = len(kv)
    per_block = keys // blocks
    width = wo.shape[0]
    steps = keys // KEY_STEP
    scale = HEAD ** (-0.5)

    def body(place_ref, seen_ref, own_ref, other_ref, q_ref, o_ref, lse_ref, mask_ref, cos_ref, sin_ref, wo_ref, *rest):
        kv_refs = rest[:blocks]
        go_ref, dq_ref = rest[blocks : blocks + 2]
        dkv_refs = rest[blocks + 2 : 2 * blocks + 2]
        kv_all, dkv_all, acc, do_all, kv_sems, d_sems = rest[2 * blocks + 2 :]
        kv_copies = fetch(
            kv_refs, [kv_all.at[:, pl.ds(j * per_block, per_block), :] for j in range(blocks)], kv_sems
        )
        t = place_ref[2]
        go_ref[t] = own_ref[...]
        go_ref[1 - t] = other_ref[...]
        for copy in kv_copies:
            copy.wait()
        for m in range(micro):
            do = mm(go_ref[m], wo_ref[...]).astype(bf16)
            pieces = []
            for h in range(heads):
                do_h = do[:, h * HEAD : (h + 1) * HEAD]
                do_all[h * rows : (h + 1) * rows, :] = do_h
                product = do_h.astype(f32) * o_ref[m, :, h * HEAD : (h + 1) * HEAD].astype(f32)
                pieces.append(jnp.sum(product.T, 0, keepdims=True))
            delta = jnp.concatenate(pieces, 1)
            acc[...] = jnp.zeros_like(acc)
            queries, outs, total = q_ref[m], do_all[...], lse_ref[m]

            def step(n, carry, m=m, queries=queries, outs=outs, total=total, delta=delta):
                start = pl.multiple_of(n * KEY_STEP, KEY_STEP)
                span = pl.ds(start, KEY_STEP)

                @pl.when(seen_ref[m * steps + n] > 0)
                def _():
                    keys_n = kv_all[m, span, :HEAD]
                    values_n = kv_all[m, span, HEAD:]
                    bias = mask_ref[m, span, :].astype(f32)
                    scores = mm(keys_n, queries, NT) * scale + jnp.concatenate([bias] * heads, 1)
                    probs = jnp.exp(scores - total)
                    ds = (probs * (mm(values_n, outs, NT) - delta)).astype(bf16)
                    acc[...] += mm(keys_n, ds, TN)
                    dkv_all[m, span, :HEAD] = (mm(ds, queries) * scale).astype(bf16)
                    dkv_all[m, span, HEAD:] = mm(probs.astype(bf16), outs).astype(bf16)

                @pl.when(seen_ref[m * steps + n] == 0)
                def _():
                    dkv_all[m, span, :] = jnp.zeros((KEY_STEP, 2 * HEAD), bf16)

                return carry

            lax.fori_loop(0, steps, step, 0)
            for h in range(heads):
                back = acc[:, h * rows : (h + 1) * rows].T * scale
                part = slice(m * rows, (m + 1) * rows)
                dq_ref[part, h * HEAD : (h + 1) * HEAD] = rotated(
                    back, cos_ref[part, :], -sin_ref[part, :]
                ).astype(bf16)
        d_copies = fetch(
            [dkv_all.at[:, pl.ds(j * per_block, per_block), :] for j in range(blocks)], dkv_refs, d_sems
        )
        for copy in d_copies:
            copy.wait()

    return pl.pallas_call(
        body,
        name="attend_back",
        out_shape=(
            shape((micro, rows, width), bf16),
            shape((micro * rows, heads * HEAD), bf16),
            *[shape((micro, per_block, 2 * HEAD), bf16)] * blocks,
        ),
        in_specs=scalars() * 2 + vmem(9) + anywhere(blocks),
        out_specs=(*vmem(2), *anywhere(blocks)),
        scratch_shapes=[
            pltpu.VMEM((micro, keys, 2 * HEAD), bf16),
            pltpu.VMEM((micro, keys, 2 * HEAD), bf16),
            pltpu.VMEM((HEAD, stacked), f32),
            pltpu.VMEM((stacked, HEAD), bf16),
            pltpu.SemaphoreType.DMA((blocks,)),
            pltpu.SemaphoreType.DMA((blocks,)),
        ],
        compiler_params=params(),
        cost_estimate=cost(
            2 * micro * stacked * keys * HEAD * 5,
            2 * micro * keys * 4 * HEAD + 2 * width * heads * HEAD,
        ),
    )(place, seen, go_own, go_other, q, o, lse, mask, cosine, sine, wo, *kv)


def project_back(dkv, dq, cosine, sine, w):
    count = len(dkv)
    micro, rows, _ = dkv[0].shape
    width, columns = w.shape
    wide = columns - 2 * HEAD

    def body(*refs):
        dq_ref, cos_ref, sin_ref, w_ref, dkv_ref, da_ref = refs[count:]
        for m in range(micro):
            part = slice(m * rows, (m + 1) * rows)
            total = refs[0][m].astype(f32)
            for ref in refs[1:count]:
                total += ref[m].astype(f32)
            dkv_ref[part, :HEAD] = rotated(
                total[:, :HEAD], cos_ref[part, :], -sin_ref[part, :]
            ).astype(bf16)
            dkv_ref[part, HEAD:] = total[:, HEAD:].astype(bf16)
            da_ref[m] = (
                mm(dq_ref[part, :], w_ref[:, :wide], NT) + mm(dkv_ref[part, :], w_ref[:, wide:], NT)
            ).astype(bf16)

    return pl.pallas_call(
        body,
        name="project_back",
        out_shape=(shape((micro * rows, 2 * HEAD), bf16), shape((micro, rows, width), bf16)),
        in_specs=vmem(count + 4),
        out_specs=tuple(vmem(2)),
        compiler_params=params(),
        cost_estimate=cost(2 * micro * rows * width * columns, 2 * width * columns),
    )(*dkv, dq, cosine, sine, w)


def first_norm_back(place, da, other, x, gain, dmiddle, lane_at):
    rows, width = dmiddle.shape

    def body(place_ref, da_ref, other_ref, x_ref, gain_ref, dmiddle_ref, ig_ref, small_ref):
        t = place_ref[2]
        total = da_ref[t].astype(f32) + other_ref[...].astype(f32)
        values = x_ref[t].astype(f32)
        scale = norm_scale(values)
        normal = values * scale
        dn = total * gain_ref[...]
        ig_ref[...] = dmiddle_ref[...] + scale * (
            dn - normal * jnp.mean(dn * normal, -1, keepdims=True)
        )
        lane = lax.broadcasted_iota(jnp.int32, (rows, LANES), 1)
        small_ref[...] = mm(total * normal, (lane == lane_at).astype(f32), TN, EXACT)

    return pl.pallas_call(
        body,
        name="first_norm_back",
        out_shape=(shape((rows, width), f32), shape((width, LANES), f32)),
        in_specs=scalars() + vmem(5),
        out_specs=tuple(vmem(2)),
        compiler_params=params(),
        cost_estimate=cost(2 * 6 * rows * width * LANES, 20 * rows * width),
    )(place, da, other, x, gain, dmiddle)


def solution(mesh):
    F, C, T = mesh.shape["fsdp"], mesh.shape["ctx"], mesh.shape["tp"]

    def local(
        tokens,
        gain_attn,
        w_query,
        w_key,
        w_value,
        w_output,
        gain_mlp,
        w_router,
        w_gate,
        w_up,
        w_down,
        lineage,
        expert_ids,
        cotangent,
    ):
        micro, rows, width = tokens.shape
        depth = width // F
        experts = w_router.shape[1]
        local_experts = experts // C
        slots = lineage.shape[2]
        f, c, t = lax.axis_index("fsdp"), lax.axis_index("ctx"), lax.axis_index("tp")
        place = jnp.stack([f, c, t]).astype(jnp.int32)

        def pick(pair, index):
            return jnp.where(index == 0, pair[0], pair[1])

        def core(value):
            return swap(value, "tp", T, 1)

        small = jnp.concatenate(
            [gain_attn[None, :], gain_mlp[None, :], w_router.T, jnp.zeros((6, depth), bf16)], 0
        )
        small = exchange_direct([small] * F, "fsdp", F)
        in_cols = jnp.concatenate([w_query, w_key, w_value], 1)
        half = in_cols.shape[1] // 2
        in_a = gather_relative(in_cols[:, :half], "fsdp", F, True)
        in_b = gather_relative(in_cols[:, half:], "fsdp", F, False)
        in_weights = [block for pair in zip(in_a, in_b) for block in pair]
        out_rows = w_output.T
        half = out_rows.shape[1] // 2
        out_a = gather_relative(out_rows[:, :half], "fsdp", F, True)
        out_b = gather_relative(out_rows[:, half:], "fsdp", F, False)
        out_weights = [block for pair in zip(out_a, out_b) for block in pair]
        first = c * local_experts
        mine = [lax.dynamic_slice_in_dim(w, first, local_experts, 0) for w in (w_gate, w_up, w_down)]
        expert_weights = []
        for e in range(local_experts):
            own = jnp.stack([mine[0][e], mine[1][e], mine[2][e].T])
            expert_weights.append(gather_relative(own, "fsdp", F, e % 2 == 0))
        gains = jnp.concatenate(small, 1)
        gain_one, gain_two = gains[0:1].astype(f32), gains[1:2].astype(f32)
        router = jnp.pad(gains[2 : 2 + experts].T, ((0, 0), (0, LANES - experts)))

        x = lanes_relative(tokens, f, F)
        c_mine = lanes_relative(pick(cotangent, t), f, F)
        ids_mine = pick(expert_ids, t)
        chosen = jnp.sum(
            (ids_mine[:, :, None] == jnp.arange(LANES, dtype=jnp.int32)[None, None, :]).astype(f32), 1
        ).astype(bf16)
        cx_mine = jnp.concatenate([c_mine, chosen], 1)

        def to_rows(mine_value):
            got = jnp.stack(exchange_direct([mine_value] * C, "ctx", C))
            both = jnp.stack([got, core(got)])
            return both.reshape(T * C * rows // MOE_ROWS, MOE_ROWS, mine_value.shape[-1])

        cx_rows = to_rows(cx_mine)

        f_order = f ^ jnp.arange(F, dtype=jnp.int32)
        c_order = c ^ jnp.arange(C, dtype=jnp.int32)
        block_order = (f_order[:, None] * C + c_order[None, :]).reshape(-1)
        key_index = (block_order[:, None] * rows + jnp.arange(rows, dtype=jnp.int32)).reshape(-1)
        key_owner = lineage[:, 0].reshape(micro, F, C, rows)
        key_owner = axis_relative(axis_relative(key_owner, 1, f), 2, c).reshape(micro, slots)
        first_row = (f * C + c) * rows
        query_lin = lax.dynamic_slice_in_dim(lineage, first_row, rows, 2)
        query_index = first_row + jnp.arange(rows, dtype=jnp.int32)
        owner = key_owner[:, :, None]
        visible = (
            ((owner == query_lin[:, 0, None, :]) & (key_index[None, :, None] <= query_index))
            | (owner == query_lin[:, 1, None, :])
            | (owner == query_lin[:, 2, None, :])
        )
        mask = jnp.where(visible, 0.0, NEG_FILL).astype(bf16)
        counts = jnp.sum(visible.astype(f32).reshape(micro, slots // KEY_STEP, KEY_STEP, rows), 2)
        positions = (jnp.sum(counts, 1) - 1.0).reshape(micro * rows)
        seen = (jnp.max(counts, -1) > 0).astype(jnp.int32).reshape(-1)
        frequency = ROPE_BASE ** (-jnp.arange(HEAD // 2, dtype=f32) / (HEAD // 2))
        angles = positions[:, None] * frequency[None, :]
        cosine, sine = jnp.cos(angles), jnp.sin(angles)
        cosine = jnp.concatenate([cosine, cosine], 1)
        sine = jnp.concatenate([-sine, sine], 1)

        a, q, kv_own, in_all = project_in(
            x.reshape(micro * rows, width), gain_one, cosine, sine, in_weights, micro, rows
        )
        kv_ctx = jnp.concatenate(exchange_direct([kv_own] * C, "ctx", C), 1)
        kv = exchange_direct([kv_ctx] * F, "fsdp", F)
        branch, o, lse, wo_all = attend(seen, q, mask, kv, out_weights)
        middle, b = second_norm(place, x, branch, core(pick(branch, 1 - t)), gain_two)

        b_rows = to_rows(b)
        out_parts, back_parts, *grads = experts_step(
            place, b_rows, cx_rows, router, expert_weights, experts
        )

        def to_owner(parts):
            parts = parts.reshape(T, C, rows, parts.shape[-1])
            got = core(parts[1])
            return exchange_direct([add_low(parts[0, k], got[k]) for k in range(C)], "ctx", C)

        dmiddle, go, small_grad = second_norm_back(
            to_owner(back_parts), middle, b, cx_mine, gain_two, router, experts
        )
        out_sums = to_owner(out_parts)
        result = middle
        for part in out_sums:
            result = result + part.astype(f32)
        result = result.astype(bf16)

        expert_grads = []
        for e in range(local_experts):
            expert_grads.append(
                scatter_relative(grads[e * F : (e + 1) * F], "fsdp", F, e % 2 == 0)
            )
        expert_grads = lax.all_gather(jnp.stack(expert_grads), "ctx", axis=0, tiled=True)

        go_all, dq, *dkv = attend_back(
            place, seen, go, core(go), q, o, lse, mask, cosine, sine, wo_all, kv
        )
        go_flat, o_flat = go_all.reshape(micro * rows, width), o.reshape(micro * rows, -1)

        def grad_blocks(left, right):
            return [
                mm(left[:, j * depth : (j + 1) * depth], right, TN).astype(bf16) for j in range(F)
            ]

        def over_ctx(part):
            step = part.shape[0] // C
            pieces = [lax.dynamic_slice_in_dim(part, (c ^ k) * step, step, 0) for k in range(C)]
            got = exchange_direct(pieces, "ctx", C)
            total = got[0].astype(f32)
            for piece in got[1:]:
                total = total + piece.astype(f32)
            total = total.astype(bf16)
            return jnp.concatenate(ordered(exchange_direct([total] * C, "ctx", C), c), 0)

        grad_out = over_ctx(scatter_relative(grad_blocks(go_flat, o_flat), "fsdp", F, True))
        dkv = exchange_direct(dkv, "fsdp", F)
        total = dkv[0].astype(f32)
        for part in dkv[1:]:
            total = total + part.astype(f32)
        total = total.astype(bf16).reshape(micro, C, rows, 2 * HEAD)
        dkv = exchange_direct([total[:, k] for k in range(C)], "ctx", C)
        dkv, da = project_back(dkv, dq, cosine, sine, in_all)
        grad_q = over_ctx(scatter_relative(grad_blocks(a, dq), "fsdp", F, False))
        input_grad, small_more = first_norm_back(
            place, da, core(pick(da, 1 - t)), x, gain_one, dmiddle, experts + 1
        )
        small_grad = small_grad + small_more
        small_grad = (small_grad + core(small_grad)).astype(bf16)
        tail = [
            jnp.concatenate([block, small_grad[j * depth : (j + 1) * depth]], 1)
            for j, block in enumerate(grad_blocks(a, dkv))
        ]
        grad_tail = over_ctx(scatter_relative(tail, "fsdp", F, True)).astype(f32)

        def whole(mine_value):
            other = core(mine_value)
            both = jnp.stack([pick((mine_value, other), t), pick((other, mine_value), t)])
            return lanes_relative(both, f, F)

        return (
            whole(result),
            whole(input_grad),
            grad_tail[:, 2 * HEAD + experts + 1],
            grad_q.astype(f32),
            grad_tail[:, :HEAD],
            grad_tail[:, HEAD : 2 * HEAD],
            grad_out.astype(f32).T,
            grad_tail[:, 2 * HEAD + experts],
            grad_tail[:, 2 * HEAD : 2 * HEAD + experts],
            expert_grads[:, 0].astype(f32),
            expert_grads[:, 1].astype(f32),
            jnp.swapaxes(expert_grads[:, 2].astype(f32), 1, 2),
        )

    rows_of = P(None, ("fsdp", "ctx"), None)
    weights = (
        P("fsdp"),
        P("fsdp", "tp"),
        P("fsdp", "tp"),
        P("fsdp", "tp"),
        P("tp", "fsdp"),
        P("fsdp"),
        P("fsdp", None),
        P(None, "fsdp", "tp"),
        P(None, "fsdp", "tp"),
        P(None, "tp", "fsdp"),
    )
    return jax.shard_map(
        local,
        mesh=mesh,
        in_specs=(rows_of, *weights, P(), rows_of, rows_of),
        out_specs=(rows_of, rows_of, *weights),
        check_vma=False,
    )
```

```python
import jax
import jax.numpy as jnp
from jax import lax
from jax.experimental import pallas as pl
from jax.experimental.pallas import tpu as pltpu
from jax.sharding import PartitionSpec as P

HEAD = 128
LANES = 128
EPSILON = 1e-06
ROPE_BASE = 1000000.0
NEG_FILL = -1e30
KEY_STEP = 256
MOE_ROWS = 512
SLICES = 2
VMEM_BYTES = 60 * 2**20

f32 = jnp.float32
bf16 = jnp.bfloat16
EXACT = lax.Precision.HIGHEST
NN = (((1,), (0,)), ((), ()))
NT = (((1,), (1,)), ((), ()))
TN = (((0,), (0,)), ((), ()))


def mm(left, right, dims=NN, precision=None):
    return lax.dot_general(left, right, dims, precision=precision, preferred_element_type=f32)


def vmem(count):
    return [pl.BlockSpec(memory_space=pltpu.VMEM)] * count


def anywhere(count):
    return [pl.BlockSpec(memory_space=pl.ANY)] * count


def scalars():
    return [pl.BlockSpec(memory_space=pltpu.SMEM)]


def shape(dims, kind):
    return jax.ShapeDtypeStruct(dims, kind)


def cost(flops, moved):
    return pl.CostEstimate(flops=int(flops), bytes_accessed=int(moved), transcendentals=0)


def params():
    return pltpu.CompilerParams(vmem_limit_bytes=VMEM_BYTES)


def swap(value, axis, size, bit):
    return lax.ppermute(value, axis, [(i, i ^ bit) for i in range(size)])


def low_bit(number):
    return number & -number


def high_bit(number):
    return 1 << (number.bit_length() - 1)


def after(value, *earlier):
    return lax.optimization_barrier((value, *earlier))[0]


def gather_first(own, axis, size):
    return [
        own if j == 0 else swap(own, axis, size, j) if low_bit(j) == high_bit(j) else None
        for j in range(size)
    ]


def gather_rest(got, axis, size, dim=0, ties=()):
    rows, got = got[0].shape[dim], list(got)

    def half(j, top):
        if isinstance(got[j], tuple):
            return got[j][0 if top else 1]
        begin = 0 if top else rows // 2
        return after(lax.slice_in_dim(got[j], begin, begin + rows // 2, axis=dim), *ties)

    for j in range(1, size):
        low, high = low_bit(j), high_bit(j)
        if low != high:
            got[j] = (
                swap(half(j ^ high, True), axis, size, high),
                swap(half(j ^ low, False), axis, size, low),
            )
    return [
        (piece, j * rows + row)
        for j, block in enumerate(got)
        for piece, row in (
            ((block[0], 0), (block[1], rows // 2)) if isinstance(block, tuple) else ((block, 0),)
        )
    ]


def held_pieces(pieces, others):
    arrays, others = lax.optimization_barrier(([array for array, _ in pieces], others))
    return [(array, row) for array, (_, row) in zip(arrays, pieces)], others


def add_low(left, right):
    return (left.astype(f32) + right.astype(f32)).astype(bf16)


def scatter_order(size, high):
    bits = size.bit_length() - 1
    if high:
        return list(range(size))
    return [sum(((n >> k) & 1) << (bits - 1 - k) for k in range(bits)) for n in range(size)]


def scatter_bits(size, high):
    bits = [1 << k for k in range(size.bit_length() - 1)]
    return bits[::-1] if high else bits


def scatter_first(send, axis, size, high):
    return swap(send, axis, size, scatter_bits(size, high)[0])


def scatter_rest(keep, got, axis, size, high):
    for bit in scatter_bits(size, high)[1:]:
        count = keep.shape[0] // 2
        send = add_low(keep[count:], got[count:])
        keep, got = add_low(keep[:count], got[:count]), swap(send, axis, size, bit)
    return add_low(keep[0], got[0])


def exchange_direct(blocks, axis, size):
    return [blocks[0]] + [swap(blocks[j], axis, size, j) for j in range(1, size)]


def ordered(blocks, index):
    count = len(blocks)
    bit = 1
    while bit < count:
        flag = (index & bit) != 0
        blocks = [jnp.where(flag, blocks[i ^ bit], blocks[i]) for i in range(count)]
        bit *= 2
    return blocks


def axis_relative(value, dim, index):
    count, bit, dims = value.shape[dim], 1, value.shape
    while bit < count:
        split = value.reshape(*dims[:dim], count // (2 * bit), 2, bit, *dims[dim + 1 :])
        value = jnp.where((index & bit) != 0, jnp.flip(split, dim + 1), split).reshape(dims)
        bit *= 2
    return value


def lanes_relative(value, index, count):
    width = value.shape[-1] // count
    return jnp.concatenate(
        [
            lax.dynamic_slice_in_dim(value, (index ^ j) * width, width, value.ndim - 1)
            for j in range(count)
        ],
        -1,
    )


def rotated(values, cosine, sine):
    return values * cosine + pltpu.roll(values, HEAD // 2, 1) * sine


def norm_scale(values):
    return lax.rsqrt(jnp.mean(values * values, -1, keepdims=True) + EPSILON)


def fetch(sources, targets, sems):
    copies = [
        pltpu.make_async_copy(source, target, sems.at[number])
        for number, (source, target) in enumerate(zip(sources, targets))
    ]
    for copy in copies:
        copy.start()
    return copies


def project_in(x, cosine, sine, pieces, micro, rows, experts):
    total, width = x.shape
    parts = len(pieces)
    columns = pieces[0][0].shape[1] - LANES
    heads = (columns - 2 * HEAD) // HEAD

    def body(x_ref, cos_ref, sin_ref, *rest):
        w_refs, (a_ref, q_ref, kv_ref, all_ref, small_ref, gains_ref, sems) = rest[:parts], rest[parts:]
        copies = fetch(
            w_refs,
            [all_ref.at[pl.ds(row, array.shape[0]), :] for array, row in pieces],
            sems,
        )
        values = x_ref[...].astype(f32)
        normal = values * norm_scale(values)
        for copy in copies:
            copy.wait()
        small = all_ref[:, columns:]
        small_ref[...] = small
        gains = small.astype(f32).T[experts : experts + 8, :]
        gains_ref[...] = gains
        a_ref[...] = (normal * gains[0:1, :]).astype(bf16)
        for m in range(micro):
            span = slice(m * rows, (m + 1) * rows)
            mixed = mm(a_ref[span, :], all_ref[:, :columns])
            cosine_m, sine_m = cos_ref[span, :], sin_ref[span, :]
            for h in range(heads):
                q_ref[m, h * rows : (h + 1) * rows, :] = rotated(
                    mixed[:, h * HEAD : (h + 1) * HEAD], cosine_m, sine_m
                ).astype(bf16)
            kv_ref[m, :, :HEAD] = rotated(
                mixed[:, heads * HEAD : (heads + 1) * HEAD], cosine_m, sine_m
            ).astype(bf16)
            kv_ref[m, :, HEAD:] = mixed[:, (heads + 1) * HEAD :].astype(bf16)

    return pl.pallas_call(
        body,
        name="project_in",
        out_shape=(
            shape((total, width), bf16),
            shape((micro, heads * rows, HEAD), bf16),
            shape((micro, rows, 2 * HEAD), bf16),
            shape((width, columns + LANES), bf16),
            shape((width, LANES), bf16),
            shape((8, width), f32),
        ),
        in_specs=vmem(3) + anywhere(parts),
        out_specs=tuple(vmem(6)),
        scratch_shapes=[pltpu.SemaphoreType.DMA((parts,))],
        compiler_params=params(),
        cost_estimate=cost(2 * total * width * columns, 4 * width * columns),
    )(x, cosine, sine, *[array for array, _ in pieces])


def attend(seen, q, mask, kv, weights):
    micro, stacked, _ = q.shape
    keys, rows = mask.shape[1], mask.shape[2]
    heads = stacked // rows
    blocks, parts = len(kv), len(weights)
    width = sum(array.shape[0] for array, _ in weights)
    steps = keys // KEY_STEP
    scale = HEAD ** (-0.5)

    def body(seen_ref, q_ref, mask_ref, *rest):
        kv_refs, w_refs = rest[:blocks], rest[blocks : blocks + parts]
        branch_ref, o_ref, lse_ref, wo_ref, kv_all, top, total, acc, kv_sems, w_sems = rest[
            blocks + parts :
        ]
        kv_copies = fetch(
            kv_refs, [kv_all.at[:, pl.ds(row, array.shape[1]), :] for array, row in kv], kv_sems
        )
        w_copies = fetch(
            w_refs, [wo_ref.at[pl.ds(row, array.shape[0]), :] for array, row in weights], w_sems
        )
        for copy in kv_copies:
            copy.wait()
        for m in range(micro):
            top[...] = jnp.full_like(top, NEG_FILL)
            total[...] = jnp.zeros_like(total)
            acc[...] = jnp.zeros_like(acc)
            queries = q_ref[m]

            def step(n, carry, m=m, queries=queries):
                @pl.when(seen_ref[m * steps + n] > 0)
                def _():
                    start = pl.multiple_of(n * KEY_STEP, KEY_STEP)
                    keys_n = kv_all[m, pl.ds(start, KEY_STEP), :HEAD]
                    values_n = kv_all[m, pl.ds(start, KEY_STEP), HEAD:]
                    bias = mask_ref[m, pl.ds(start, KEY_STEP), :].astype(f32)
                    scores = mm(keys_n, queries, NT) * scale + jnp.concatenate([bias] * heads, 1)
                    peak = jnp.maximum(top[...], jnp.max(scores, 0, keepdims=True))
                    rescale = jnp.exp(top[...] - peak)
                    weights_n = jnp.exp(scores - peak)
                    total[...] = total[...] * rescale + jnp.sum(weights_n, 0, keepdims=True)
                    acc[...] = acc[...] * rescale + mm(values_n, weights_n.astype(bf16), TN)
                    top[...] = peak

                return carry

            lax.fori_loop(0, steps, step, 0)
            lse_ref[m] = top[...] + jnp.log(total[...])
            mixed = acc[...] / total[...]
            for h in range(heads):
                o_ref[m, :, h * HEAD : (h + 1) * HEAD] = mixed[
                    :, h * rows : (h + 1) * rows
                ].T.astype(bf16)
        for copy in w_copies:
            copy.wait()
        for m in range(micro):
            branch_ref[m] = mm(o_ref[m], wo_ref[...], NT).astype(bf16)

    return pl.pallas_call(
        body,
        name="attend",
        out_shape=(
            shape((micro, rows, width), bf16),
            shape((micro, rows, heads * HEAD), bf16),
            shape((micro, 1, stacked), f32),
            shape((width, heads * HEAD), bf16),
        ),
        in_specs=scalars() + vmem(2) + anywhere(blocks + parts),
        out_specs=tuple(vmem(4)),
        scratch_shapes=[
            pltpu.VMEM((micro, keys, 2 * HEAD), bf16),
            pltpu.VMEM((1, stacked), f32),
            pltpu.VMEM((1, stacked), f32),
            pltpu.VMEM((HEAD, stacked), f32),
            pltpu.SemaphoreType.DMA((blocks,)),
            pltpu.SemaphoreType.DMA((parts,)),
        ],
        compiler_params=params(),
        cost_estimate=cost(
            2 * micro * stacked * keys * HEAD * 2 + 2 * micro * rows * width * heads * HEAD,
            2 * micro * keys * 2 * HEAD + 2 * width * heads * HEAD * 2,
        ),
    )(seen, q, mask, *[array for array, _ in kv], *[array for array, _ in weights])


def second_norm(place, x, branch, other, gain):
    rows, width = other.shape

    def body(place_ref, x_ref, branch_ref, other_ref, gain_ref, middle_ref, b_ref):
        t = place_ref[2]
        middle = (
            x_ref[t].astype(f32) + branch_ref[t].astype(f32) + other_ref[...].astype(f32)
        )
        middle_ref[...] = middle
        b_ref[...] = (middle * norm_scale(middle) * gain_ref[1:2, :]).astype(bf16)

    return pl.pallas_call(
        body,
        name="second_norm",
        out_shape=(shape((rows, width), f32), shape((rows, width), bf16)),
        in_specs=scalars() + vmem(4),
        out_specs=tuple(vmem(2)),
        compiler_params=params(),
        cost_estimate=cost(10 * rows * width, 20 * rows * width),
    )(place, x, branch, other, gain)


def routing(b, router, experts):
    logits = mm(b, router)
    lane = lax.broadcasted_iota(jnp.int32, logits.shape, 1)
    logits = jnp.where(lane < experts, logits, NEG_FILL)
    powers = jnp.exp(logits - jnp.max(logits, -1, keepdims=True))
    return powers / jnp.sum(powers, -1, keepdims=True), lane


def experts_rows(place, b, at, block, cx, router, weights, experts):
    pieces, width = len(at), b[0].shape[1]
    total = pieces * block
    rows = min(MOE_ROWS, total)
    local, _, _, hidden = weights[0][0].shape
    wide = local * hidden
    w_count = len(weights)
    half_rows = total // 2
    k0 = 0.7978845608028654
    k1 = 0.044715

    def body(place_ref, router_ref, *rest):
        b_refs, cx_refs = rest[: len(b)], rest[len(b) : 2 * len(b)]
        w_refs, rest = rest[2 * len(b) : 2 * len(b) + w_count], rest[2 * len(b) + w_count :]
        out_refs, back_refs, (scaled_ref, gate_ref, up_ref) = rest[:2], rest[2:4], rest[4:7]
        b_all, cx_all, w_all, b_sems, cx_sems, w_sems = rest[7:]
        row_copies = fetch(
            [b_refs[n % len(b)].at[pl.ds(row, block), :] for n, row in enumerate(at)],
            [b_all.at[pl.ds(n * block, block), :] for n in range(pieces)],
            b_sems,
        )
        w_copies = fetch(
            [ref.at[e] for ref in w_refs for e in range(local)],
            [
                w_all.at[:, pl.ds(row, array.shape[2]), pl.ds(e * hidden, hidden)]
                for array, row in weights
                for e in range(local)
            ],
            w_sems,
        )
        row_copies += fetch(
            [cx_refs[n % len(b)].at[pl.ds(row, block), :] for n, row in enumerate(at)],
            [cx_all.at[pl.ds(n * block, block), :] for n in range(pieces)],
            cx_sems,
        )
        for copy in row_copies:
            copy.wait()
        lane = lax.broadcasted_iota(jnp.int32, (rows, LANES), 1)
        for start in range(0, total, rows):
            span = slice(start, start + rows)
            probs, _ = routing(b_all[span, :], router_ref[...], experts)
            gates = probs * cx_all[span, width:].astype(f32)
            mine = [lane == place_ref[1] * local + e for e in range(local)]
            gate = jnp.concatenate(
                [
                    jnp.broadcast_to(
                        jnp.sum(jnp.where(mine[e], gates, 0.0), -1, keepdims=True), (rows, hidden)
                    )
                    for e in range(local)
                ],
                1,
            )
            if start == 0:
                for copy in w_copies:
                    copy.wait()
            b_rows = b_all[span, :]
            z = mm(b_rows, w_all[0])
            up = mm(b_rows, w_all[1])
            down_back = mm(cx_all[span, :width], w_all[2])
            square = z * z
            bend = jnp.tanh(k0 * z * (1.0 + k1 * square))
            half = 0.5 * (1.0 + bend)
            active = z * half
            slope = half + 0.5 * z * (1.0 - bend * bend) * (k0 * (1.0 + 3.0 * k1 * square))
            hidden_rows = active * up
            hidden_back = gate * down_back
            scaled_ref[span, :] = (gate * hidden_rows).astype(bf16)
            gate_ref[span, :] = (hidden_back * up * slope).astype(bf16)
            up_ref[span, :] = (hidden_back * active).astype(bf16)
            product = hidden_rows * down_back
            share = jnp.zeros((rows, LANES), f32)
            for e in range(local):
                share += jnp.where(
                    mine[e],
                    jnp.sum(product[:, e * hidden : (e + 1) * hidden], -1, keepdims=True),
                    0.0,
                )
            out = mm(scaled_ref[span, :], w_all[2], NT).astype(bf16)
            back = (
                mm(gate_ref[span, :], w_all[0], NT) + mm(up_ref[span, :], w_all[1], NT)
            ).astype(bf16)
            share = share.astype(bf16)
            for n in range(2):
                low, high = max(start, n * half_rows), min(start + rows, (n + 1) * half_rows)
                if low < high:
                    to = slice(low - n * half_rows, high - n * half_rows)
                    out_refs[n][to, :] = out[low - start : high - start]
                    back_refs[n][to, :width] = back[low - start : high - start]
                    back_refs[n][to, width:] = share[low - start : high - start]

    return pl.pallas_call(
        body,
        name="experts_rows",
        out_shape=(
            *[shape((half_rows, width), bf16)] * 2,
            *[shape((half_rows, width + LANES), bf16)] * 2,
            *[shape((total, wide), bf16)] * 3,
        ),
        in_specs=scalars() + vmem(1) + anywhere(2 * len(b) + w_count),
        out_specs=tuple(vmem(7)),
        scratch_shapes=[
            pltpu.VMEM((total, width), bf16),
            pltpu.VMEM((total, width + LANES), bf16),
            pltpu.VMEM((3, width, wide), bf16),
            pltpu.SemaphoreType.DMA((pieces,)),
            pltpu.SemaphoreType.DMA((pieces,)),
            pltpu.SemaphoreType.DMA((local * w_count,)),
        ],
        compiler_params=params(),
        cost_estimate=cost(12 * total * width * wide, 2 * (4 * total * width + 3 * width * wide)),
    )(place, router, *b, *cx, *[array for array, _ in weights])


def experts_grads(b, cx, at, block, sides, local, parts):
    pieces, width = len(at), b[0].shape[1]
    total = pieces * block
    calls = len(sides)
    each = total // calls
    wide = sides[0][0].shape[1]
    hidden, depth, half = wide // local, width // parts, parts // 2
    fine = depth // 2
    orders = [scatter_order(parts, n == 0) for n in range(2)]

    def body(*refs):
        b_refs, cx_refs, side_refs = refs[: len(b)], refs[len(b) : 2 * len(b)], refs[2 * len(b) :]
        side_refs, rest = side_refs[: 3 * calls], side_refs[3 * calls :]
        grad_refs = rest[:4]
        b_all, c_all, side_all, turned, stage, b_sems, c_sems, s_sems, g_sems = rest[4:]
        b_copies = fetch(
            [b_refs[n % len(b)].at[pl.ds(row, block), :] for n, row in enumerate(at)],
            [b_all.at[pl.ds(n * block, block), :] for n in range(pieces)],
            b_sems,
        )
        s_copies = fetch(
            side_refs,
            [
                side_all.at[n, pl.ds(call * each, each), :]
                for call in range(calls)
                for n in range(3)
            ],
            s_sems,
        )
        c_copies = fetch(
            [
                cx_refs[n % len(b)].at[pl.ds(row, block), pl.ds(0, width)]
                for n, row in enumerate(at)
            ],
            [c_all.at[pl.ds(n * block, block), :] for n in range(pieces)],
            c_sems,
        )
        for copy in b_copies + s_copies:
            copy.wait()
        g_copies = []
        for n, side in ((0, 1), (1, 2), (2, 0)):
            if n == 0:
                turned[...] = b_all[...].T
            if n == 2:
                for copy in c_copies:
                    copy.wait()
                turned[...] = c_all[...].T
            for j in range(parts):
                span = slice(j * depth, (j + 1) * depth)
                stage[n, span, :] = mm(turned[span, :], side_all[side]).astype(bf16)
                for e in range(local):
                    for way in range(2):
                        to = orders[way].index(j)
                        copy = pltpu.make_async_copy(
                            stage.at[
                                n, pl.ds(j * depth + way * fine, fine), pl.ds(e * hidden, hidden)
                            ],
                            grad_refs[2 * way + to // half].at[to % half, e, n],
                            g_sems.at[len(g_copies)],
                        )
                        copy.start()
                        g_copies.append(copy)
        for copy in g_copies:
            copy.wait()

    return pl.pallas_call(
        body,
        name="experts_grads",
        out_shape=tuple([shape((half, local, 3, fine, hidden), bf16)] * 4),
        in_specs=anywhere(2 * len(b) + 3 * calls),
        out_specs=tuple(anywhere(4)),
        scratch_shapes=[
            pltpu.VMEM((total, width), bf16),
            pltpu.VMEM((total, width), bf16),
            pltpu.VMEM((3, total, wide), bf16),
            pltpu.VMEM((width, total), bf16),
            pltpu.VMEM((3, width, wide), bf16),
            pltpu.SemaphoreType.DMA((pieces,)),
            pltpu.SemaphoreType.DMA((pieces,)),
            pltpu.SemaphoreType.DMA((3 * calls,)),
            pltpu.SemaphoreType.DMA((3 * parts * local * 2,)),
        ],
        compiler_params=params(),
        cost_estimate=cost(
            6 * total * width * wide, 2 * (2 * total * width + 3 * total * wide + 3 * width * wide)
        ),
    )(*b, *cx, *[array for side in sides for array in side])


def second_norm_back(sums, middle, b, cx, gain, router, experts):
    rows, width = middle.shape
    slices, count = len(sums), len(sums[0])
    part = rows // slices

    def body(*refs):
        sum_refs, refs = refs[: slices * count], refs[slices * count :]
        middle_ref, b_ref, cx_ref, gain_ref, router_ref, dmiddle_ref, go_ref, dl_ref, dgain_ref = refs
        weights = router_ref[...]
        for n in range(slices):
            span = slice(n * part, (n + 1) * part)
            total = sum_refs[n * count][...].astype(f32)
            for ref in sum_refs[n * count + 1 : (n + 1) * count]:
                total += ref[...].astype(f32)
            b_rows = b_ref[span, :]
            share = total[:, width:] * cx_ref[span, width:].astype(f32)
            probs, _ = routing(b_rows, weights, experts)
            dl = probs * (share - jnp.sum(probs * share, -1, keepdims=True))
            dl_high = dl.astype(bf16)
            dl_low = (dl - dl_high.astype(f32)).astype(bf16)
            db = total[:, :width] + mm(dl_high, weights, NT) + mm(dl_low, weights, NT)
            values = middle_ref[span, :]
            scale = norm_scale(values)
            normal = values * scale
            dn = db * gain_ref[1:2, :]
            dmiddle = cx_ref[span, :width].astype(f32) + scale * (
                dn - normal * jnp.mean(dn * normal, -1, keepdims=True)
            )
            dmiddle_ref[span, :] = dmiddle
            go_ref[span, :] = dmiddle.astype(bf16)
            dl_ref[span, :] = dl_high
            dgain_ref[span, :] = (db * normal).astype(bf16)

    return pl.pallas_call(
        body,
        name="second_norm_back",
        out_shape=(
            shape((rows, width), f32),
            shape((rows, width), bf16),
            shape((rows, LANES), bf16),
            shape((rows, width), bf16),
        ),
        in_specs=vmem(slices * count + 5),
        out_specs=tuple(vmem(4)),
        compiler_params=params(),
        cost_estimate=cost(2 * 20 * rows * width * LANES, 24 * rows * width),
    )(*[part for one in sums for part in one], middle, b, cx, gain, router)


def attend_back(place, seen, go_own, go_other, q, o, lse, mask, cosine, sine, wo, kv, groups):
    micro, stacked, _ = q.shape
    keys, rows = mask.shape[1], mask.shape[2]
    heads = stacked // rows
    blocks = len(kv)
    per_group = keys // groups
    width = wo.shape[0]
    steps = keys // KEY_STEP
    scale = HEAD ** (-0.5)

    def body(place_ref, seen_ref, own_ref, other_ref, q_ref, o_ref, lse_ref, mask_ref, cos_ref, sin_ref, wo_ref, *rest):
        kv_refs = rest[:blocks]
        go_ref, dq_ref = rest[blocks : blocks + 2]
        dkv_refs = rest[blocks + 2 : blocks + groups + 2]
        kv_all, dkv_all, acc, do_all, kv_sems, d_sems = rest[blocks + groups + 2 :]
        kv_copies = fetch(
            kv_refs, [kv_all.at[:, pl.ds(row, array.shape[1]), :] for array, row in kv], kv_sems
        )
        t = place_ref[2]
        go_ref[t] = own_ref[...]
        go_ref[1 - t] = other_ref[...]
        for copy in kv_copies:
            copy.wait()
        for m in range(micro):
            do = mm(go_ref[m], wo_ref[...]).astype(bf16)
            pieces = []
            for h in range(heads):
                do_h = do[:, h * HEAD : (h + 1) * HEAD]
                do_all[h * rows : (h + 1) * rows, :] = do_h
                product = do_h.astype(f32) * o_ref[m, :, h * HEAD : (h + 1) * HEAD].astype(f32)
                pieces.append(jnp.sum(product.T, 0, keepdims=True))
            delta = jnp.concatenate(pieces, 1)
            acc[...] = jnp.zeros_like(acc)
            queries, outs, total = q_ref[m], do_all[...], lse_ref[m]

            def step(n, carry, m=m, queries=queries, outs=outs, total=total, delta=delta):
                start = pl.multiple_of(n * KEY_STEP, KEY_STEP)
                span = pl.ds(start, KEY_STEP)

                @pl.when(seen_ref[m * steps + n] > 0)
                def _():
                    keys_n = kv_all[m, span, :HEAD]
                    values_n = kv_all[m, span, HEAD:]
                    bias = mask_ref[m, span, :].astype(f32)
                    scores = mm(keys_n, queries, NT) * scale + jnp.concatenate([bias] * heads, 1)
                    probs = jnp.exp(scores - total)
                    ds = (probs * (mm(values_n, outs, NT) - delta)).astype(bf16)
                    acc[...] += mm(keys_n, ds, TN)
                    dkv_all[m, span, :HEAD] = (mm(ds, queries) * scale).astype(bf16)
                    dkv_all[m, span, HEAD:] = mm(probs.astype(bf16), outs).astype(bf16)

                @pl.when(seen_ref[m * steps + n] == 0)
                def _():
                    dkv_all[m, span, :] = jnp.zeros((KEY_STEP, 2 * HEAD), bf16)

                return carry

            lax.fori_loop(0, steps, step, 0)
            for h in range(heads):
                back = acc[:, h * rows : (h + 1) * rows].T * scale
                part = slice(m * rows, (m + 1) * rows)
                dq_ref[part, h * HEAD : (h + 1) * HEAD] = rotated(
                    back, cos_ref[part, :], -sin_ref[part, :]
                ).astype(bf16)
        d_copies = fetch(
            [dkv_all.at[:, pl.ds(j * per_group, per_group), :] for j in range(groups)], dkv_refs, d_sems
        )
        for copy in d_copies:
            copy.wait()

    return pl.pallas_call(
        body,
        name="attend_back",
        out_shape=(
            shape((micro, rows, width), bf16),
            shape((micro * rows, heads * HEAD), bf16),
            *[shape((micro, per_group, 2 * HEAD), bf16)] * groups,
        ),
        in_specs=scalars() * 2 + vmem(9) + anywhere(blocks),
        out_specs=(*vmem(2), *anywhere(groups)),
        scratch_shapes=[
            pltpu.VMEM((micro, keys, 2 * HEAD), bf16),
            pltpu.VMEM((micro, keys, 2 * HEAD), bf16),
            pltpu.VMEM((HEAD, stacked), f32),
            pltpu.VMEM((stacked, HEAD), bf16),
            pltpu.SemaphoreType.DMA((blocks,)),
            pltpu.SemaphoreType.DMA((groups,)),
        ],
        compiler_params=params(),
        cost_estimate=cost(
            2 * micro * stacked * keys * HEAD * 5,
            2 * micro * keys * 4 * HEAD + 2 * width * heads * HEAD,
        ),
    )(place, seen, go_own, go_other, q, o, lse, mask, cosine, sine, wo, *[array for array, _ in kv])


def project_back(dkv, dq, cosine, sine, w):
    count = len(dkv)
    micro, rows, _ = dkv[0].shape
    width, columns = w.shape
    columns -= LANES
    wide = columns - 2 * HEAD

    def body(*refs):
        dq_ref, cos_ref, sin_ref, w_ref, dkv_ref, da_ref = refs[count:]
        for m in range(micro):
            part = slice(m * rows, (m + 1) * rows)
            total = refs[0][m].astype(f32)
            for ref in refs[1:count]:
                total += ref[m].astype(f32)
            dkv_ref[part, :HEAD] = rotated(
                total[:, :HEAD], cos_ref[part, :], -sin_ref[part, :]
            ).astype(bf16)
            dkv_ref[part, HEAD:] = total[:, HEAD:].astype(bf16)
            da_ref[m] = (
                mm(dq_ref[part, :], w_ref[:, :wide], NT) + mm(dkv_ref[part, :], w_ref[:, wide:columns], NT)
            ).astype(bf16)

    return pl.pallas_call(
        body,
        name="project_back",
        out_shape=(shape((micro * rows, 2 * HEAD), bf16), shape((micro, rows, width), bf16)),
        in_specs=vmem(count + 4),
        out_specs=tuple(vmem(2)),
        compiler_params=params(),
        cost_estimate=cost(2 * micro * rows * width * columns, 2 * width * columns),
    )(*dkv, dq, cosine, sine, w)


def first_norm_back(place, da, other, x, gain, dmiddle):
    rows, width = dmiddle.shape

    def body(place_ref, da_ref, other_ref, x_ref, gain_ref, dmiddle_ref, ig_ref, dgain_ref):
        t = place_ref[2]
        total = da_ref[t].astype(f32) + other_ref[...].astype(f32)
        values = x_ref[t].astype(f32)
        scale = norm_scale(values)
        normal = values * scale
        dn = total * gain_ref[0:1, :]
        ig_ref[...] = dmiddle_ref[...] + scale * (
            dn - normal * jnp.mean(dn * normal, -1, keepdims=True)
        )
        dgain_ref[...] = (total * normal).astype(bf16)

    return pl.pallas_call(
        body,
        name="first_norm_back",
        out_shape=(shape((rows, width), f32), shape((rows, width), bf16)),
        in_specs=scalars() + vmem(5),
        out_specs=tuple(vmem(2)),
        compiler_params=params(),
        cost_estimate=cost(2 * 6 * rows * width * LANES, 20 * rows * width),
    )(place, da, other, x, gain, dmiddle)


def assemble(gathered):
    count, _, local, _, fine, hidden = gathered.shape
    depth = 2 * fine

    def body(in_ref, gate_ref, up_ref, down_ref):
        for way in range(2):
            span = slice(way * fine, (way + 1) * fine)
            gate_ref[0, span, :] = in_ref[0, way, 0, 0].astype(f32)
            up_ref[0, span, :] = in_ref[0, way, 0, 1].astype(f32)
            down_ref[0, :, span] = in_ref[0, way, 0, 2].astype(f32).T

    at = lambda j, e: (j * local + e, 0, 0)
    return pl.pallas_call(
        body,
        name="assemble",
        grid=(count, local),
        in_specs=[
            pl.BlockSpec((1, 2, 1, 3, fine, hidden), lambda j, e: (j, 0, e, 0, 0, 0))
        ],
        out_specs=(
            pl.BlockSpec((1, depth, hidden), at),
            pl.BlockSpec((1, depth, hidden), at),
            pl.BlockSpec((1, hidden, depth), at),
        ),
        out_shape=(
            *[shape((count * local, depth, hidden), f32)] * 2,
            shape((count * local, hidden, depth), f32),
        ),
        compiler_params=params(),
        cost_estimate=cost(count * local * depth * hidden * 3, count * local * depth * hidden * 18),
    )(gathered)


def attention_grads(a, go, dq, dkv, o, b, dl, dgain_one, dgain_two, experts, parts):
    rows, width = a.shape
    depth = width // parts
    half = parts // 2
    lanes = (dq.shape[1] + dkv.shape[1], o.shape[1] + LANES)

    def body(a_ref, go_ref, dq_ref, dkv_ref, o_ref, b_ref, dl_ref, one_ref, two_ref, *out_refs):
        def put(n, lane, total):
            for to, j in enumerate(scatter_order(parts, n == 0)):
                out_refs[2 * n + to // half][to % half, :, lane : lane + total.shape[1]] = total[
                    j * depth : (j + 1) * depth
                ].astype(bf16)

        turned = a_ref[...].T
        put(0, 0, mm(turned, dq_ref[...]))
        put(0, dq_ref.shape[1], mm(turned, dkv_ref[...]))
        put(1, 0, mm(go_ref[...].T, o_ref[...]))
        lane = lax.broadcasted_iota(jnp.int32, dl_ref.shape, 1)
        put(
            1,
            o_ref.shape[1],
            mm(b_ref[...].T, dl_ref[...])
            + mm(one_ref[...].T, (lane == experts).astype(bf16))
            + mm(two_ref[...].T, (lane == experts + 1).astype(bf16)),
        )

    return pl.pallas_call(
        body,
        name="attention_grads",
        out_shape=tuple(shape((half, depth, lanes[n // 2]), bf16) for n in range(4)),
        in_specs=vmem(9),
        out_specs=tuple(vmem(4)),
        compiler_params=params(),
        cost_estimate=cost(2 * rows * width * sum(lanes), 2 * width * sum(lanes)),
    )(a, go, dq, dkv, o, b, dl, dgain_one, dgain_two)


def solution(mesh):
    F, C, T = mesh.shape["fsdp"], mesh.shape["ctx"], mesh.shape["tp"]

    def local(
        tokens,
        gain_attn,
        w_query,
        w_key,
        w_value,
        w_output,
        gain_mlp,
        w_router,
        w_gate,
        w_up,
        w_down,
        lineage,
        expert_ids,
        cotangent,
    ):
        micro, rows, width = tokens.shape
        depth = width // F
        experts = w_router.shape[1]
        local_experts = experts // C
        slots = lineage.shape[2]
        f, c, t = lax.axis_index("fsdp"), lax.axis_index("ctx"), lax.axis_index("tp")
        place = jnp.stack([f, c, t]).astype(jnp.int32)

        def pick(pair, index):
            return jnp.where(index == 0, pair[0], pair[1])

        def core(value):
            return swap(value, "tp", T, 1)

        small = jnp.concatenate(
            [
                w_router,
                gain_attn[:, None],
                gain_mlp[:, None],
                jnp.zeros((depth, LANES - experts - 2), bf16),
            ],
            1,
        )
        in_own = jnp.concatenate([w_query, w_key, w_value, small], 1)

        def experts_of(index):
            mine = [
                lax.dynamic_slice_in_dim(w, index * local_experts, local_experts, 0)
                for w in (w_gate, w_up, w_down)
            ]
            return jnp.stack([mine[0], mine[1], jnp.swapaxes(mine[2], 1, 2)], 1)

        expert_own = experts_of(c)

        x = lanes_relative(tokens, f, F)
        c_mine = lanes_relative(pick(cotangent, t), f, F)
        ids_mine = pick(expert_ids, t)
        chosen = jnp.sum(
            (ids_mine[:, :, None] == jnp.arange(LANES, dtype=jnp.int32)[None, None, :]).astype(f32), 1
        ).astype(bf16)
        cx_mine = jnp.concatenate([c_mine, chosen], 1)

        f_order = f ^ jnp.arange(F, dtype=jnp.int32)
        c_order = c ^ jnp.arange(C, dtype=jnp.int32)
        block_order = (f_order[:, None] * C + c_order[None, :]).reshape(-1)
        key_index = (block_order[:, None] * rows + jnp.arange(rows, dtype=jnp.int32)).reshape(-1)
        key_owner = lineage[:, 0].reshape(micro, F, C, rows)
        key_owner = axis_relative(axis_relative(key_owner, 1, f), 2, c).reshape(micro, slots)
        first_row = (f * C + c) * rows
        query_lin = lax.dynamic_slice_in_dim(lineage, first_row, rows, 2)
        query_index = first_row + jnp.arange(rows, dtype=jnp.int32)
        owner = key_owner[:, :, None]
        visible = (
            ((owner == query_lin[:, 0, None, :]) & (key_index[None, :, None] <= query_index))
            | (owner == query_lin[:, 1, None, :])
            | (owner == query_lin[:, 2, None, :])
        )
        mask = jnp.where(visible, 0.0, NEG_FILL).astype(bf16)
        counts = jnp.sum(visible.astype(f32).reshape(micro, slots // KEY_STEP, KEY_STEP, rows), 2)
        positions = (jnp.sum(counts, 1) - 1.0).reshape(micro * rows)
        seen = (jnp.max(counts, -1) > 0).astype(jnp.int32).reshape(-1)
        frequency = ROPE_BASE ** (-jnp.arange(HEAD // 2, dtype=f32) / (HEAD // 2))
        angles = positions[:, None] * frequency[None, :]
        cosine, sine = jnp.cos(angles), jnp.sin(angles)
        cosine = jnp.concatenate([cosine, cosine], 1)
        sine = jnp.concatenate([-sine, sine], 1)

        hold = lax.optimization_barrier
        far = C // 2
        in_first = gather_first(in_own, "fsdp", F)
        in_first, mask, cosine, sine, seen, x = hold((in_first, mask, cosine, sine, seen, x))
        in_pieces = gather_rest(in_first, "fsdp", F)
        in_pieces, (out_own, cx_mine, expert_own) = held_pieces(
            in_pieces, (w_output.T, cx_mine, expert_own)
        )
        out_there = exchange_direct([out_own] * F, "fsdp", F)
        a, q, kv_own, in_all, router, gains = project_in(
            x.reshape(micro * rows, width), cosine, sine, in_pieces, micro, rows, experts
        )
        kv_ctx = jnp.concatenate(exchange_direct([kv_own] * C, "ctx", C), 1)
        kv_ctx, out_there, cx_mine = hold((kv_ctx, out_there, cx_mine))
        out_pieces = [(array, j * depth) for j, array in enumerate(out_there)]
        kv = exchange_direct([kv_ctx] * F, "fsdp", F)
        cx_there = [
            cx_mine if k == 0 else None if k == far else swap(cx_mine, "ctx", C, k)
            for k in range(C)
        ]
        cx_far, kv, cx_there, expert_own = hold((cx_mine, kv, cx_there, expert_own))
        kv = [(array, j * C * rows) for j, array in enumerate(kv)]
        expert_first = gather_first(expert_own, "fsdp", F)
        cx_there[far] = swap(cx_far, "ctx", C, far)
        branch, o, lse, wo_all = attend(seen, q, mask, kv, out_pieces)
        cx_other = [core(block) if k != far else None for k, block in enumerate(cx_there)]
        middle, b = second_norm(place, x, branch, core(pick(branch, 1 - t)), gains)
        b, middle, cx_there, cx_other = hold((b, middle, cx_there, cx_other))

        there = exchange_direct([b] * C, "ctx", C)
        expert_pieces = gather_rest(expert_first, "fsdp", F, 2)
        expert_there = [block for block in expert_first if block is not None]
        there, cx_there[far] = after((there, cx_there[far]), *expert_there)
        cx_other[far] = core(cx_there[far])
        cx_both = cx_there + cx_other
        b_both = there + [core(block) for block in there]
        part = rows // SLICES

        def to_sums(own, other):
            got = core(other)
            return [
                add_low(own[k * part : (k + 1) * part], got[k * part : (k + 1) * part])
                for k in range(C)
            ]

        outs, back_sums, sides = [], [], []
        sums = None
        for n in range(SLICES):
            out_mine, out_other, back_mine, back_other, *side = experts_rows(
                place,
                b_both,
                [n * part] * (2 * C),
                part,
                cx_both,
                after(router, *sums) if sums else router,
                expert_pieces,
                experts,
            )
            outs.append((out_mine, out_other))
            sides.append(side)
            sums = to_sums(back_mine, back_other)
            back_sums.append(exchange_direct(sums, "ctx", C))
        b_at = [n * part for n in range(SLICES) for _ in b_both]
        sides, _, outs = hold((sides, sums, outs))
        grads = experts_grads(b_both, cx_both, b_at, part, sides, local_experts, F)
        out_sums = [
            jnp.concatenate(pieces, 0) for pieces in zip(*[to_sums(*pair) for pair in outs])
        ]
        back_sums, grads, out_sums = hold((back_sums, grads, out_sums))

        def first_round(pieces):
            return [scatter_first(pieces[2 * n + 1], "fsdp", F, n == 0) for n in range(2)]

        def other_rounds(pieces, got):
            return [scatter_rest(pieces[2 * n], got[n], "fsdp", F, n == 0) for n in range(2)]

        grads_got = first_round(grads)
        for k in range(1, C):
            if k != far:
                out_sums[k] = swap(out_sums[k], "ctx", C, k)
        dmiddle, go, dl, dgain_two = second_norm_back(
            back_sums, middle, b, cx_mine, gains, router, experts
        )
        go_all, dq, *dkv = attend_back(
            place, seen, go, core(go), q, o, lse, mask, cosine, sine, wo_all, kv, F
        )
        go_all, dq, dkv, out_sums = hold((go_all, dq, dkv, out_sums))
        go_flat, o_flat = go_all.reshape(micro * rows, width), o.reshape(micro * rows, -1)

        dkv = exchange_direct(dkv, "fsdp", F)
        out_sums[far] = swap(out_sums[far], "ctx", C, far)
        total = dkv[0].astype(f32)
        for piece in dkv[1:]:
            total = total + piece.astype(f32)
        total = total.astype(bf16).reshape(micro, C, rows, 2 * HEAD)
        total, grads_got, out_sums = hold((total, grads_got, out_sums))
        grad_own = other_rounds(grads, grads_got)
        dkv = exchange_direct([total[:, k] for k in range(C)], "ctx", C)
        dkv, grad_own = hold((dkv, jnp.stack(grad_own)))
        gathered = lax.all_gather(grad_own, "ctx", axis=0)
        dkv, da = project_back(dkv, dq, cosine, sine, in_all)
        input_grad, dgain_one = first_norm_back(
            place, da, core(pick(da, 1 - t)), x, gains, dmiddle
        )
        attn_grads = attention_grads(
            a, go_flat, dq, dkv, o_flat, b, dl, dgain_one, dgain_two, experts, F
        )
        attn_got = first_round(attn_grads)
        pieces = other_rounds(attn_grads, attn_got)
        step = depth // C
        pieces = jnp.concatenate(pieces, 1)
        got = exchange_direct(
            [lax.dynamic_slice_in_dim(pieces, (c ^ k) * step, step, 0) for k in range(C)], "ctx", C
        )
        wide = w_query.shape[1]
        total = got[0].astype(f32)
        for piece in got[1:]:
            total = total + piece.astype(f32)
        total = total.astype(bf16)
        tail = total[:, wide + 2 * HEAD + o_flat.shape[1] :]
        total = jnp.concatenate([total[:, : wide + 2 * HEAD + o_flat.shape[1]], add_low(tail, core(tail))], 1)
        got = exchange_direct([total] * C, "ctx", C)
        grad_gate, grad_up, grad_down = assemble(gathered)
        grad_all = jnp.concatenate(ordered(got, c), 0).astype(f32)
        grad_q, grad_k, grad_v = jnp.split(grad_all[:, : wide + 2 * HEAD], (wide, wide + HEAD), 1)
        grad_out, grad_small = jnp.split(grad_all[:, wide + 2 * HEAD :], (o_flat.shape[1],), 1)
        result = sum((piece.astype(f32) for piece in out_sums), middle).astype(bf16)

        def whole(mine_value):
            other = core(mine_value)
            both = jnp.stack([pick((mine_value, other), t), pick((other, mine_value), t)])
            return lanes_relative(both, f, F)

        return (
            whole(result),
            whole(input_grad),
            grad_small[:, experts],
            grad_q,
            grad_k,
            grad_v,
            grad_out.T,
            grad_small[:, experts + 1],
            grad_small[:, :experts],
            grad_gate,
            grad_up,
            grad_down,
        )

    rows_of = P(None, ("fsdp", "ctx"), None)
    weights = (
        P("fsdp"),
        P("fsdp", "tp"),
        P("fsdp", "tp"),
        P("fsdp", "tp"),
        P("tp", "fsdp"),
        P("fsdp"),
        P("fsdp", None),
        P(None, "fsdp", "tp"),
        P(None, "fsdp", "tp"),
        P(None, "tp", "fsdp"),
    )
    return jax.shard_map(
        local,
        mesh=mesh,
        in_specs=(rows_of, *weights, P(), rows_of, rows_of),
        out_specs=(rows_of, rows_of, *weights),
        check_vma=False,
    )
```

```python
import jax
import jax.numpy as jnp
from jax import lax
from jax.experimental import pallas as pl
from jax.experimental.pallas import tpu as pltpu
from jax.sharding import PartitionSpec as P

HEAD = 128
LANES = 128
EPSILON = 1e-06
ROPE_BASE = 1000000.0
NEG_FILL = -1e30
KEY_STEP = 256
MOE_ROWS = 512
SLICES = 1
VMEM_BYTES = 60 * 2**20

f32 = jnp.float32
bf16 = jnp.bfloat16
EXACT = lax.Precision.HIGHEST
NN = (((1,), (0,)), ((), ()))
NT = (((1,), (1,)), ((), ()))
TN = (((0,), (0,)), ((), ()))


def mm(left, right, dims=NN, precision=None):
    return lax.dot_general(left, right, dims, precision=precision, preferred_element_type=f32)


def vmem(count):
    return [pl.BlockSpec(memory_space=pltpu.VMEM)] * count


def anywhere(count):
    return [pl.BlockSpec(memory_space=pl.ANY)] * count


def scalars():
    return [pl.BlockSpec(memory_space=pltpu.SMEM)]


def shape(dims, kind):
    return jax.ShapeDtypeStruct(dims, kind)


def cost(flops, moved):
    return pl.CostEstimate(flops=int(flops), bytes_accessed=int(moved), transcendentals=0)


def params():
    return pltpu.CompilerParams(vmem_limit_bytes=VMEM_BYTES)


def swap(value, axis, size, bit):
    return lax.ppermute(value, axis, [(i, i ^ bit) for i in range(size)])


def low_bit(number):
    return number & -number


def high_bit(number):
    return 1 << (number.bit_length() - 1)


def after(value, *earlier):
    return lax.optimization_barrier((value, *earlier))[0]


def gather_first(own, axis, size):
    return [
        own if j == 0 else swap(own, axis, size, j) if low_bit(j) == high_bit(j) else None
        for j in range(size)
    ]


def gather_first_halves(own, axis, size):
    rows = own.shape[0] // 2
    halves = (own[:rows], own[rows:])
    return [
        halves
        if j == 0
        else tuple(swap(half, axis, size, j) for half in halves)
        if low_bit(j) == high_bit(j)
        else None
        for j in range(size)
    ]


def gather_rest(got, axis, size, dim=0, ties=()):
    got = list(got)
    rows = 2 * got[0][0].shape[dim] if isinstance(got[0], tuple) else got[0].shape[dim]

    def half(j, top):
        if isinstance(got[j], tuple):
            return got[j][0 if top else 1]
        begin = 0 if top else rows // 2
        return after(lax.slice_in_dim(got[j], begin, begin + rows // 2, axis=dim), *ties)

    for j in range(1, size):
        low, high = low_bit(j), high_bit(j)
        if low != high:
            got[j] = (
                swap(half(j ^ high, True), axis, size, high),
                swap(half(j ^ low, False), axis, size, low),
            )
    return [
        (piece, j * rows + row)
        for j, block in enumerate(got)
        for piece, row in (
            ((block[0], 0), (block[1], rows // 2)) if isinstance(block, tuple) else ((block, 0),)
        )
    ]


def held_pieces(pieces, others):
    arrays, others = lax.optimization_barrier(([array for array, _ in pieces], others))
    return [(array, row) for array, (_, row) in zip(arrays, pieces)], others


def add_low(left, right):
    return (left.astype(f32) + right.astype(f32)).astype(bf16)


def scatter_order(size, high):
    bits = size.bit_length() - 1
    if high:
        return list(range(size))
    return [sum(((n >> k) & 1) << (bits - 1 - k) for k in range(bits)) for n in range(size)]


def scatter_bits(size, high):
    bits = [1 << k for k in range(size.bit_length() - 1)]
    return bits[::-1] if high else bits


def scatter_first(send, axis, size, high):
    return swap(send, axis, size, scatter_bits(size, high)[0])


def scatter_rest(keep, got, axis, size, high):
    for bit in scatter_bits(size, high)[1:]:
        count = keep.shape[0] // 2
        send = add_low(keep[count:], got[count:])
        keep, got = add_low(keep[:count], got[:count]), swap(send, axis, size, bit)
    return add_low(keep[0], got[0])


def exchange_direct(blocks, axis, size):
    return [blocks[0]] + [swap(blocks[j], axis, size, j) for j in range(1, size)]


def axis_relative(value, dim, index):
    count, bit, dims = value.shape[dim], 1, value.shape
    while bit < count:
        split = value.reshape(*dims[:dim], count // (2 * bit), 2, bit, *dims[dim + 1 :])
        value = jnp.where((index & bit) != 0, jnp.flip(split, dim + 1), split).reshape(dims)
        bit *= 2
    return value


def lanes_relative(value, index, count):
    width = value.shape[-1] // count
    return jnp.concatenate(
        [
            lax.dynamic_slice_in_dim(value, (index ^ j) * width, width, value.ndim - 1)
            for j in range(count)
        ],
        -1,
    )


def rotated(values, cosine, sine):
    return values * cosine + pltpu.roll(values, HEAD // 2, 1) * sine


def norm_scale(values):
    return lax.rsqrt(jnp.mean(values * values, -1, keepdims=True) + EPSILON)


def fetch(sources, targets, sems):
    copies = [
        pltpu.make_async_copy(source, target, sems.at[number])
        for number, (source, target) in enumerate(zip(sources, targets))
    ]
    for copy in copies:
        copy.start()
    return copies


def project_in(x, cosine, sine, pieces, micro, rows, experts):
    total, width = x.shape
    parts = len(pieces)
    columns = pieces[0][0].shape[1] - LANES
    heads = (columns - 2 * HEAD) // HEAD

    def body(x_ref, cos_ref, sin_ref, *rest):
        w_refs, (a_ref, q_ref, kv_ref, all_ref, small_ref, gains_ref, sems) = rest[:parts], rest[parts:]
        copies = fetch(
            w_refs,
            [all_ref.at[pl.ds(row, array.shape[0]), :] for array, row in pieces],
            sems,
        )
        values = x_ref[...].astype(f32)
        normal = values * norm_scale(values)
        for copy in copies:
            copy.wait()
        small = all_ref[:, columns:]
        small_ref[...] = small
        gains = small.astype(f32).T[experts : experts + 8, :]
        gains_ref[...] = gains
        a_ref[...] = (normal * gains[0:1, :]).astype(bf16)
        for m in range(micro):
            span = slice(m * rows, (m + 1) * rows)
            mixed = mm(a_ref[span, :], all_ref[:, :columns])
            cosine_m, sine_m = cos_ref[span, :], sin_ref[span, :]
            for h in range(heads):
                q_ref[m, h * rows : (h + 1) * rows, :] = rotated(
                    mixed[:, h * HEAD : (h + 1) * HEAD], cosine_m, sine_m
                ).astype(bf16)
            kv_ref[m, :, :HEAD] = rotated(
                mixed[:, heads * HEAD : (heads + 1) * HEAD], cosine_m, sine_m
            ).astype(bf16)
            kv_ref[m, :, HEAD:] = mixed[:, (heads + 1) * HEAD :].astype(bf16)

    return pl.pallas_call(
        body,
        name="project_in",
        out_shape=(
            shape((total, width), bf16),
            shape((micro, heads * rows, HEAD), bf16),
            shape((micro, rows, 2 * HEAD), bf16),
            shape((width, columns + LANES), bf16),
            shape((width, LANES), bf16),
            shape((8, width), f32),
        ),
        in_specs=vmem(3) + anywhere(parts),
        out_specs=tuple(vmem(6)),
        scratch_shapes=[pltpu.SemaphoreType.DMA((parts,))],
        compiler_params=params(),
        cost_estimate=cost(2 * total * width * columns, 4 * width * columns),
    )(x, cosine, sine, *[array for array, _ in pieces])


def attend(seen, q, mask, kv, weights):
    micro, stacked, _ = q.shape
    keys, rows = mask.shape[1], mask.shape[2]
    heads = stacked // rows
    blocks, parts = len(kv), len(weights)
    width = sum(array.shape[0] for array, _ in weights)
    steps = keys // KEY_STEP
    scale = HEAD ** (-0.5)

    def body(seen_ref, q_ref, mask_ref, *rest):
        kv_refs, w_refs = rest[:blocks], rest[blocks : blocks + parts]
        branch_ref, o_ref, lse_ref, wo_ref, kv_all, top, total, acc, kv_sems, w_sems = rest[
            blocks + parts :
        ]
        kv_copies = fetch(
            kv_refs, [kv_all.at[:, pl.ds(row, array.shape[1]), :] for array, row in kv], kv_sems
        )
        w_copies = fetch(
            w_refs, [wo_ref.at[pl.ds(row, array.shape[0]), :] for array, row in weights], w_sems
        )
        for copy in kv_copies:
            copy.wait()
        for m in range(micro):
            top[...] = jnp.full_like(top, NEG_FILL)
            total[...] = jnp.zeros_like(total)
            acc[...] = jnp.zeros_like(acc)
            queries = q_ref[m]

            def step(n, carry, m=m, queries=queries):
                @pl.when(seen_ref[m * steps + n] > 0)
                def _():
                    start = pl.multiple_of(n * KEY_STEP, KEY_STEP)
                    keys_n = kv_all[m, pl.ds(start, KEY_STEP), :HEAD]
                    values_n = kv_all[m, pl.ds(start, KEY_STEP), HEAD:]
                    bias = mask_ref[m, pl.ds(start, KEY_STEP), :].astype(f32)
                    scores = mm(keys_n, queries, NT) * scale + jnp.concatenate([bias] * heads, 1)
                    peak = jnp.maximum(top[...], jnp.max(scores, 0, keepdims=True))
                    rescale = jnp.exp(top[...] - peak)
                    weights_n = jnp.exp(scores - peak)
                    total[...] = total[...] * rescale + jnp.sum(weights_n, 0, keepdims=True)
                    acc[...] = acc[...] * rescale + mm(values_n, weights_n.astype(bf16), TN)
                    top[...] = peak

                return carry

            lax.fori_loop(0, steps, step, 0)
            lse_ref[m] = top[...] + jnp.log(total[...])
            mixed = acc[...] / total[...]
            for h in range(heads):
                o_ref[m, :, h * HEAD : (h + 1) * HEAD] = mixed[
                    :, h * rows : (h + 1) * rows
                ].T.astype(bf16)
        for copy in w_copies:
            copy.wait()
        for m in range(micro):
            branch_ref[m] = mm(o_ref[m], wo_ref[...], NT).astype(bf16)

    return pl.pallas_call(
        body,
        name="attend",
        out_shape=(
            shape((micro, rows, width), bf16),
            shape((micro, rows, heads * HEAD), bf16),
            shape((micro, 1, stacked), f32),
            shape((width, heads * HEAD), bf16),
        ),
        in_specs=scalars() + vmem(2) + anywhere(blocks + parts),
        out_specs=tuple(vmem(4)),
        scratch_shapes=[
            pltpu.VMEM((micro, keys, 2 * HEAD), bf16),
            pltpu.VMEM((1, stacked), f32),
            pltpu.VMEM((1, stacked), f32),
            pltpu.VMEM((HEAD, stacked), f32),
            pltpu.SemaphoreType.DMA((blocks,)),
            pltpu.SemaphoreType.DMA((parts,)),
        ],
        compiler_params=params(),
        cost_estimate=cost(
            2 * micro * stacked * keys * HEAD * 2 + 2 * micro * rows * width * heads * HEAD,
            2 * micro * keys * 2 * HEAD + 2 * width * heads * HEAD * 2,
        ),
    )(seen, q, mask, *[array for array, _ in kv], *[array for array, _ in weights])


def second_norm(place, x, branch, other, gain):
    rows, width = other.shape

    def body(place_ref, x_ref, branch_ref, other_ref, gain_ref, middle_ref, b_ref):
        t = place_ref[2]
        middle = (
            x_ref[t].astype(f32) + branch_ref[t].astype(f32) + other_ref[...].astype(f32)
        )
        middle_ref[...] = middle
        b_ref[...] = (middle * norm_scale(middle) * gain_ref[1:2, :]).astype(bf16)

    return pl.pallas_call(
        body,
        name="second_norm",
        out_shape=(shape((rows, width), f32), shape((rows, width), bf16)),
        in_specs=scalars() + vmem(4),
        out_specs=tuple(vmem(2)),
        compiler_params=params(),
        cost_estimate=cost(10 * rows * width, 20 * rows * width),
    )(place, x, branch, other, gain)


def routing(b, router, experts):
    logits = mm(b, router)
    lane = lax.broadcasted_iota(jnp.int32, logits.shape, 1)
    logits = jnp.where(lane < experts, logits, NEG_FILL)
    powers = jnp.exp(logits - jnp.max(logits, -1, keepdims=True))
    return powers / jnp.sum(powers, -1, keepdims=True), lane


def experts_rows(place, b, at, block, cx, router, weights, experts):
    pieces, width = len(at), b[0].shape[1]
    total = pieces * block
    rows = min(MOE_ROWS, total)
    local, _, _, hidden = weights[0][0].shape
    wide = local * hidden
    w_count = len(weights)
    half_rows = total // 2
    k0 = 0.7978845608028654
    k1 = 0.044715

    def body(place_ref, router_ref, *rest):
        b_refs, cx_refs = rest[: len(b)], rest[len(b) : 2 * len(b)]
        w_refs, rest = rest[2 * len(b) : 2 * len(b) + w_count], rest[2 * len(b) + w_count :]
        out_refs, back_refs, side_refs = rest[:2], rest[2:4], rest[4:7]
        b_all, cx_all, w_all, out_low, back_low, sides, b_sems, cx_sems, w_sems, o_sems = rest[7:]
        scaled_ref, gate_ref, up_ref = (sides.at[n] for n in range(3))
        o_copies = []

        def send(source, target):
            copy = pltpu.make_async_copy(source, target, o_sems.at[len(o_copies)])
            copy.start()
            o_copies.append(copy)

        row_copies = fetch(
            [b_refs[n % len(b)].at[pl.ds(row, block), :] for n, row in enumerate(at)],
            [b_all.at[pl.ds(n * block, block), :] for n in range(pieces)],
            b_sems,
        )
        w_copies = fetch(
            [ref.at[e] for ref in w_refs for e in range(local)],
            [
                w_all.at[:, pl.ds(row, array.shape[2]), pl.ds(e * hidden, hidden)]
                for array, row in weights
                for e in range(local)
            ],
            w_sems,
        )
        row_copies += fetch(
            [cx_refs[n % len(b)].at[pl.ds(row, block), :] for n, row in enumerate(at)],
            [cx_all.at[pl.ds(n * block, block), :] for n in range(pieces)],
            cx_sems,
        )
        for copy in row_copies:
            copy.wait()
        lane = lax.broadcasted_iota(jnp.int32, (rows, LANES), 1)
        for start in range(0, total, rows):
            span = slice(start, start + rows)
            probs, _ = routing(b_all[span, :], router_ref[...], experts)
            gates = probs * cx_all[span, width:].astype(f32)
            mine = [lane == place_ref[1] * local + e for e in range(local)]
            gate = jnp.concatenate(
                [
                    jnp.broadcast_to(
                        jnp.sum(jnp.where(mine[e], gates, 0.0), -1, keepdims=True), (rows, hidden)
                    )
                    for e in range(local)
                ],
                1,
            )
            if start == 0:
                for copy in w_copies:
                    copy.wait()
            b_rows = b_all[span, :]
            z = mm(b_rows, w_all[0])
            up = mm(b_rows, w_all[1])
            down_back = mm(cx_all[span, :width], w_all[2])
            square = z * z
            bend = jnp.tanh(k0 * z * (1.0 + k1 * square))
            half = 0.5 * (1.0 + bend)
            active = z * half
            slope = half + 0.5 * z * (1.0 - bend * bend) * (k0 * (1.0 + 3.0 * k1 * square))
            hidden_rows = active * up
            hidden_back = gate * down_back
            scaled_ref[span, :] = (gate * hidden_rows).astype(bf16)
            gate_ref[span, :] = (hidden_back * up * slope).astype(bf16)
            up_ref[span, :] = (hidden_back * active).astype(bf16)
            product = hidden_rows * down_back
            share = jnp.zeros((rows, LANES), f32)
            for e in range(local):
                share += jnp.where(
                    mine[e],
                    jnp.sum(product[:, e * hidden : (e + 1) * hidden], -1, keepdims=True),
                    0.0,
                )
            for n in range(3):
                send(sides.at[n, pl.ds(start, rows), :], side_refs[n].at[pl.ds(start, rows), :])
            out_low[span, :] = mm(scaled_ref[span, :], w_all[2], NT).astype(bf16)
            back_low[span, :width] = (
                mm(gate_ref[span, :], w_all[0], NT) + mm(up_ref[span, :], w_all[1], NT)
            ).astype(bf16)
            back_low[span, width:] = share.astype(bf16)
            for n in range(2):
                low, high = max(start, n * half_rows), min(start + rows, (n + 1) * half_rows)
                if low < high:
                    to = pl.ds(low - n * half_rows, high - low)
                    send(out_low.at[pl.ds(low, high - low), :], out_refs[n].at[to, :])
                    send(back_low.at[pl.ds(low, high - low), :], back_refs[n].at[to, :])
        for copy in o_copies:
            copy.wait()

    return pl.pallas_call(
        body,
        name="experts_rows",
        out_shape=(
            *[shape((half_rows, width), bf16)] * 2,
            *[shape((half_rows, width + LANES), bf16)] * 2,
            *[shape((total, wide), bf16)] * 3,
        ),
        in_specs=scalars() + vmem(1) + anywhere(2 * len(b) + w_count),
        out_specs=tuple(anywhere(7)),
        scratch_shapes=[
            pltpu.VMEM((total, width), bf16),
            pltpu.VMEM((total, width + LANES), bf16),
            pltpu.VMEM((3, width, wide), bf16),
            pltpu.VMEM((total, width), bf16),
            pltpu.VMEM((total, width + LANES), bf16),
            pltpu.VMEM((3, total, wide), bf16),
            pltpu.SemaphoreType.DMA((pieces,)),
            pltpu.SemaphoreType.DMA((pieces,)),
            pltpu.SemaphoreType.DMA((local * w_count,)),
            pltpu.SemaphoreType.DMA((7 * total // rows,)),
        ],
        compiler_params=params(),
        cost_estimate=cost(12 * total * width * wide, 2 * (4 * total * width + 3 * width * wide)),
    )(place, router, *b, *cx, *[array for array, _ in weights])


def experts_grads(b, cx, at, block, sides, local, parts):
    pieces, width = len(at), b[0].shape[1]
    total = pieces * block
    calls = len(sides)
    each = total // calls
    wide = sides[0][0].shape[1]
    hidden, depth, half = wide // local, width // parts, parts // 2
    fine = depth // 2
    orders = [scatter_order(parts, n == 0) for n in range(2)]

    def body(*refs):
        b_refs, cx_refs, side_refs = refs[: len(b)], refs[len(b) : 2 * len(b)], refs[2 * len(b) :]
        side_refs, rest = side_refs[: 3 * calls], side_refs[3 * calls :]
        grad_refs = rest[:4]
        b_all, c_all, side_all, turned, stage, b_sems, c_sems, s_sems, g_sems = rest[4:]
        b_copies = fetch(
            [b_refs[n % len(b)].at[pl.ds(row, block), :] for n, row in enumerate(at)],
            [b_all.at[pl.ds(n * block, block), :] for n in range(pieces)],
            b_sems,
        )
        s_copies = fetch(
            side_refs,
            [
                side_all.at[n, pl.ds(call * each, each), :]
                for call in range(calls)
                for n in range(3)
            ],
            s_sems,
        )
        c_copies = fetch(
            [
                cx_refs[n % len(b)].at[pl.ds(row, block), pl.ds(0, width)]
                for n, row in enumerate(at)
            ],
            [c_all.at[pl.ds(n * block, block), :] for n in range(pieces)],
            c_sems,
        )
        for copy in b_copies + s_copies:
            copy.wait()
        g_copies = []
        for n, side in ((0, 1), (1, 2), (2, 0)):
            if n == 0:
                turned[...] = b_all[...].T
            if n == 2:
                for copy in c_copies:
                    copy.wait()
                turned[...] = c_all[...].T
            for j in range(parts):
                span = slice(j * depth, (j + 1) * depth)
                stage[n, span, :] = mm(turned[span, :], side_all[side]).astype(bf16)
                for e in range(local):
                    for way in range(2):
                        to = orders[way].index(j)
                        copy = pltpu.make_async_copy(
                            stage.at[
                                n, pl.ds(j * depth + way * fine, fine), pl.ds(e * hidden, hidden)
                            ],
                            grad_refs[2 * way + to // half].at[to % half, e, n],
                            g_sems.at[len(g_copies)],
                        )
                        copy.start()
                        g_copies.append(copy)
        for copy in g_copies:
            copy.wait()

    return pl.pallas_call(
        body,
        name="experts_grads",
        out_shape=tuple([shape((half, local, 3, fine, hidden), bf16)] * 4),
        in_specs=anywhere(2 * len(b) + 3 * calls),
        out_specs=tuple(anywhere(4)),
        scratch_shapes=[
            pltpu.VMEM((total, width), bf16),
            pltpu.VMEM((total, width), bf16),
            pltpu.VMEM((3, total, wide), bf16),
            pltpu.VMEM((width, total), bf16),
            pltpu.VMEM((3, width, wide), bf16),
            pltpu.SemaphoreType.DMA((pieces,)),
            pltpu.SemaphoreType.DMA((pieces,)),
            pltpu.SemaphoreType.DMA((3 * calls,)),
            pltpu.SemaphoreType.DMA((3 * parts * local * 2,)),
        ],
        compiler_params=params(),
        cost_estimate=cost(
            6 * total * width * wide, 2 * (2 * total * width + 3 * total * wide + 3 * width * wide)
        ),
    )(*b, *cx, *[array for side in sides for array in side])


def second_norm_back(sums, middle, b, cx, gain, router, experts):
    rows, width = middle.shape
    slices, count = len(sums), len(sums[0])
    part = rows // slices

    def body(*refs):
        sum_refs, refs = refs[: slices * count], refs[slices * count :]
        middle_ref, b_ref, cx_ref, gain_ref, router_ref, dmiddle_ref, go_ref, dl_ref, dgain_ref = refs
        weights = router_ref[...]
        for n in range(slices):
            span = slice(n * part, (n + 1) * part)
            total = sum_refs[n * count][...].astype(f32)
            for ref in sum_refs[n * count + 1 : (n + 1) * count]:
                total += ref[...].astype(f32)
            b_rows = b_ref[span, :]
            share = total[:, width:] * cx_ref[span, width:].astype(f32)
            probs, _ = routing(b_rows, weights, experts)
            dl = probs * (share - jnp.sum(probs * share, -1, keepdims=True))
            dl_high = dl.astype(bf16)
            dl_low = (dl - dl_high.astype(f32)).astype(bf16)
            db = total[:, :width] + mm(dl_high, weights, NT) + mm(dl_low, weights, NT)
            values = middle_ref[span, :]
            scale = norm_scale(values)
            normal = values * scale
            dn = db * gain_ref[1:2, :]
            dmiddle = cx_ref[span, :width].astype(f32) + scale * (
                dn - normal * jnp.mean(dn * normal, -1, keepdims=True)
            )
            dmiddle_ref[span, :] = dmiddle
            go_ref[span, :] = dmiddle.astype(bf16)
            dl_ref[span, :] = dl_high
            dgain_ref[span, :] = (db * normal).astype(bf16)

    return pl.pallas_call(
        body,
        name="second_norm_back",
        out_shape=(
            shape((rows, width), f32),
            shape((rows, width), bf16),
            shape((rows, LANES), bf16),
            shape((rows, width), bf16),
        ),
        in_specs=vmem(slices * count + 5),
        out_specs=tuple(vmem(4)),
        compiler_params=params(),
        cost_estimate=cost(2 * 20 * rows * width * LANES, 24 * rows * width),
    )(*[part for one in sums for part in one], middle, b, cx, gain, router)


def attend_back(place, seen, go_own, go_other, q, o, lse, mask, cosine, sine, wo, kv, groups):
    micro, stacked, _ = q.shape
    keys, rows = mask.shape[1], mask.shape[2]
    heads = stacked // rows
    blocks = len(kv)
    per_group = keys // groups
    width = wo.shape[0]
    steps = keys // KEY_STEP
    scale = HEAD ** (-0.5)

    def body(place_ref, seen_ref, own_ref, other_ref, q_ref, o_ref, lse_ref, mask_ref, cos_ref, sin_ref, wo_ref, *rest):
        kv_refs = rest[:blocks]
        go_ref, dq_ref = rest[blocks : blocks + 2]
        dkv_refs = rest[blocks + 2 : blocks + groups + 2]
        kv_all, dkv_all, acc, do_all, kv_sems, d_sems = rest[blocks + groups + 2 :]
        kv_copies = fetch(
            kv_refs, [kv_all.at[:, pl.ds(row, array.shape[1]), :] for array, row in kv], kv_sems
        )
        t = place_ref[2]
        go_ref[t] = own_ref[...]
        go_ref[1 - t] = other_ref[...]
        for copy in kv_copies:
            copy.wait()
        for m in range(micro):
            do = mm(go_ref[m], wo_ref[...]).astype(bf16)
            pieces = []
            for h in range(heads):
                do_h = do[:, h * HEAD : (h + 1) * HEAD]
                do_all[h * rows : (h + 1) * rows, :] = do_h
                product = do_h.astype(f32) * o_ref[m, :, h * HEAD : (h + 1) * HEAD].astype(f32)
                pieces.append(jnp.sum(product.T, 0, keepdims=True))
            delta = jnp.concatenate(pieces, 1)
            acc[...] = jnp.zeros_like(acc)
            queries, outs, total = q_ref[m], do_all[...], lse_ref[m]

            def step(n, carry, m=m, queries=queries, outs=outs, total=total, delta=delta):
                start = pl.multiple_of(n * KEY_STEP, KEY_STEP)
                span = pl.ds(start, KEY_STEP)

                @pl.when(seen_ref[m * steps + n] > 0)
                def _():
                    keys_n = kv_all[m, span, :HEAD]
                    values_n = kv_all[m, span, HEAD:]
                    bias = mask_ref[m, span, :].astype(f32)
                    scores = mm(keys_n, queries, NT) * scale + jnp.concatenate([bias] * heads, 1)
                    probs = jnp.exp(scores - total)
                    ds = (probs * (mm(values_n, outs, NT) - delta)).astype(bf16)
                    acc[...] += mm(keys_n, ds, TN)
                    dkv_all[m, span, :HEAD] = (mm(ds, queries) * scale).astype(bf16)
                    dkv_all[m, span, HEAD:] = mm(probs.astype(bf16), outs).astype(bf16)

                @pl.when(seen_ref[m * steps + n] == 0)
                def _():
                    dkv_all[m, span, :] = jnp.zeros((KEY_STEP, 2 * HEAD), bf16)

                return carry

            lax.fori_loop(0, steps, step, 0)
            for h in range(heads):
                back = acc[:, h * rows : (h + 1) * rows].T * scale
                part = slice(m * rows, (m + 1) * rows)
                dq_ref[part, h * HEAD : (h + 1) * HEAD] = rotated(
                    back, cos_ref[part, :], -sin_ref[part, :]
                ).astype(bf16)
        d_copies = fetch(
            [dkv_all.at[:, pl.ds(j * per_group, per_group), :] for j in range(groups)], dkv_refs, d_sems
        )
        for copy in d_copies:
            copy.wait()

    return pl.pallas_call(
        body,
        name="attend_back",
        out_shape=(
            shape((micro, rows, width), bf16),
            shape((micro * rows, heads * HEAD), bf16),
            *[shape((micro, per_group, 2 * HEAD), bf16)] * groups,
        ),
        in_specs=scalars() * 2 + vmem(9) + anywhere(blocks),
        out_specs=(*vmem(2), *anywhere(groups)),
        scratch_shapes=[
            pltpu.VMEM((micro, keys, 2 * HEAD), bf16),
            pltpu.VMEM((micro, keys, 2 * HEAD), bf16),
            pltpu.VMEM((HEAD, stacked), f32),
            pltpu.VMEM((stacked, HEAD), bf16),
            pltpu.SemaphoreType.DMA((blocks,)),
            pltpu.SemaphoreType.DMA((groups,)),
        ],
        compiler_params=params(),
        cost_estimate=cost(
            2 * micro * stacked * keys * HEAD * 5,
            2 * micro * keys * 4 * HEAD + 2 * width * heads * HEAD,
        ),
    )(place, seen, go_own, go_other, q, o, lse, mask, cosine, sine, wo, *[array for array, _ in kv])


def project_back(dkv, dq, cosine, sine, w):
    count = len(dkv)
    micro, rows, _ = dkv[0].shape
    width, columns = w.shape
    columns -= LANES
    wide = columns - 2 * HEAD

    def body(*refs):
        dq_ref, cos_ref, sin_ref, w_ref, dkv_ref, da_ref = refs[count:]
        for m in range(micro):
            part = slice(m * rows, (m + 1) * rows)
            total = refs[0][m].astype(f32)
            for ref in refs[1:count]:
                total += ref[m].astype(f32)
            dkv_ref[part, :HEAD] = rotated(
                total[:, :HEAD], cos_ref[part, :], -sin_ref[part, :]
            ).astype(bf16)
            dkv_ref[part, HEAD:] = total[:, HEAD:].astype(bf16)
            da_ref[m] = (
                mm(dq_ref[part, :], w_ref[:, :wide], NT) + mm(dkv_ref[part, :], w_ref[:, wide:columns], NT)
            ).astype(bf16)

    return pl.pallas_call(
        body,
        name="project_back",
        out_shape=(shape((micro * rows, 2 * HEAD), bf16), shape((micro, rows, width), bf16)),
        in_specs=vmem(count + 4),
        out_specs=tuple(vmem(2)),
        compiler_params=params(),
        cost_estimate=cost(2 * micro * rows * width * columns, 2 * width * columns),
    )(*dkv, dq, cosine, sine, w)


def first_norm_back(place, da, other, x, gain, dmiddle):
    rows, width = dmiddle.shape

    def body(place_ref, da_ref, other_ref, x_ref, gain_ref, dmiddle_ref, ig_ref, dgain_ref):
        t = place_ref[2]
        total = da_ref[t].astype(f32) + other_ref[...].astype(f32)
        values = x_ref[t].astype(f32)
        scale = norm_scale(values)
        normal = values * scale
        dn = total * gain_ref[0:1, :]
        ig_ref[...] = dmiddle_ref[...] + scale * (
            dn - normal * jnp.mean(dn * normal, -1, keepdims=True)
        )
        dgain_ref[...] = (total * normal).astype(bf16)

    return pl.pallas_call(
        body,
        name="first_norm_back",
        out_shape=(shape((rows, width), f32), shape((rows, width), bf16)),
        in_specs=scalars() + vmem(5),
        out_specs=tuple(vmem(2)),
        compiler_params=params(),
        cost_estimate=cost(2 * 6 * rows * width * LANES, 20 * rows * width),
    )(place, da, other, x, gain, dmiddle)


def assemble(gathered):
    count, _, local, _, fine, hidden = gathered.shape
    depth = 2 * fine

    def body(in_ref, gate_ref, up_ref, down_ref):
        for way in range(2):
            span = slice(way * fine, (way + 1) * fine)
            gate_ref[0, span, :] = in_ref[0, way, 0, 0].astype(f32)
            up_ref[0, span, :] = in_ref[0, way, 0, 1].astype(f32)
            down_ref[0, :, span] = in_ref[0, way, 0, 2].astype(f32).T

    at = lambda j, e: (j * local + e, 0, 0)
    return pl.pallas_call(
        body,
        name="assemble",
        grid=(count, local),
        in_specs=[
            pl.BlockSpec((1, 2, 1, 3, fine, hidden), lambda j, e: (j, 0, e, 0, 0, 0))
        ],
        out_specs=(
            pl.BlockSpec((1, depth, hidden), at),
            pl.BlockSpec((1, depth, hidden), at),
            pl.BlockSpec((1, hidden, depth), at),
        ),
        out_shape=(
            *[shape((count * local, depth, hidden), f32)] * 2,
            shape((count * local, hidden, depth), f32),
        ),
        compiler_params=params(),
        cost_estimate=cost(count * local * depth * hidden * 3, count * local * depth * hidden * 18),
    )(gathered)


def assemble_attention(place, blocks, wide, out_wide):
    count = len(blocks)
    step, total = blocks[0].shape
    depth = count * step
    tail = total - wide - 2 * HEAD - out_wide

    def body(place_ref, *refs):
        q_ref, k_ref, v_ref, out_ref, small_ref, whole = refs[count:]
        for n in range(count):
            row = pl.multiple_of(lax.bitwise_xor(place_ref[1], n) * step, 8)
            whole[pl.ds(row, step), :] = refs[n][...].astype(f32)
        q_ref[...] = whole[:, :wide]
        k_ref[...] = whole[:, wide : wide + HEAD]
        v_ref[...] = whole[:, wide + HEAD : wide + 2 * HEAD]
        out_ref[...] = whole[:, wide + 2 * HEAD : wide + 2 * HEAD + out_wide].T
        small_ref[...] = whole[:, wide + 2 * HEAD + out_wide :]

    return pl.pallas_call(
        body,
        name="assemble_attention",
        out_shape=(
            shape((depth, wide), f32),
            shape((depth, HEAD), f32),
            shape((depth, HEAD), f32),
            shape((out_wide, depth), f32),
            shape((depth, tail), f32),
        ),
        in_specs=scalars() + vmem(count),
        out_specs=tuple(vmem(5)),
        scratch_shapes=[pltpu.VMEM((depth, total), f32)],
        compiler_params=params(),
        cost_estimate=cost(depth * total, 6 * depth * total),
    )(place, *blocks)


def attention_grads(a, go, dq, dkv, o, b, dl, dgain_one, dgain_two, experts, parts):
    rows, width = a.shape
    depth = width // parts
    half = parts // 2
    lanes = (dq.shape[1] + dkv.shape[1], o.shape[1] + LANES)

    def body(a_ref, go_ref, dq_ref, dkv_ref, o_ref, b_ref, dl_ref, one_ref, two_ref, *out_refs):
        def put(n, lane, total):
            for to, j in enumerate(scatter_order(parts, n == 0)):
                out_refs[2 * n + to // half][to % half, :, lane : lane + total.shape[1]] = total[
                    j * depth : (j + 1) * depth
                ].astype(bf16)

        turned = a_ref[...].T
        put(0, 0, mm(turned, dq_ref[...]))
        put(0, dq_ref.shape[1], mm(turned, dkv_ref[...]))
        put(1, 0, mm(go_ref[...].T, o_ref[...]))
        lane = lax.broadcasted_iota(jnp.int32, dl_ref.shape, 1)
        put(
            1,
            o_ref.shape[1],
            mm(b_ref[...].T, dl_ref[...])
            + mm(one_ref[...].T, (lane == experts).astype(bf16))
            + mm(two_ref[...].T, (lane == experts + 1).astype(bf16)),
        )

    return pl.pallas_call(
        body,
        name="attention_grads",
        out_shape=tuple(shape((half, depth, lanes[n // 2]), bf16) for n in range(4)),
        in_specs=vmem(9),
        out_specs=tuple(vmem(4)),
        compiler_params=params(),
        cost_estimate=cost(2 * rows * width * sum(lanes), 2 * width * sum(lanes)),
    )(a, go, dq, dkv, o, b, dl, dgain_one, dgain_two)


def solution(mesh):
    F, C, T = mesh.shape["fsdp"], mesh.shape["ctx"], mesh.shape["tp"]

    def local(
        tokens,
        gain_attn,
        w_query,
        w_key,
        w_value,
        w_output,
        gain_mlp,
        w_router,
        w_gate,
        w_up,
        w_down,
        lineage,
        expert_ids,
        cotangent,
    ):
        micro, rows, width = tokens.shape
        depth = width // F
        experts = w_router.shape[1]
        local_experts = experts // C
        slots = lineage.shape[2]
        f, c, t = lax.axis_index("fsdp"), lax.axis_index("ctx"), lax.axis_index("tp")
        place = jnp.stack([f, c, t]).astype(jnp.int32)

        def pick(pair, index):
            return jnp.where(index == 0, pair[0], pair[1])

        def core(value):
            return swap(value, "tp", T, 1)

        small = jnp.concatenate(
            [
                w_router,
                gain_attn[:, None],
                gain_mlp[:, None],
                jnp.zeros((depth, LANES - experts - 2), bf16),
            ],
            1,
        )
        in_own = jnp.concatenate([w_query, w_key, w_value, small], 1)

        def experts_of(index):
            mine = [
                lax.dynamic_slice_in_dim(w, index * local_experts, local_experts, 0)
                for w in (w_gate, w_up, w_down)
            ]
            return jnp.stack([mine[0], mine[1], jnp.swapaxes(mine[2], 1, 2)], 1)

        expert_own = experts_of(c)

        x = lanes_relative(tokens, f, F)
        c_mine = lanes_relative(pick(cotangent, t), f, F)
        ids_mine = pick(expert_ids, t)
        chosen = jnp.sum(
            (ids_mine[:, :, None] == jnp.arange(LANES, dtype=jnp.int32)[None, None, :]).astype(f32), 1
        ).astype(bf16)
        cx_mine = jnp.concatenate([c_mine, chosen], 1)

        f_order = f ^ jnp.arange(F, dtype=jnp.int32)
        c_order = c ^ jnp.arange(C, dtype=jnp.int32)
        block_order = (f_order[:, None] * C + c_order[None, :]).reshape(-1)
        key_index = (block_order[:, None] * rows + jnp.arange(rows, dtype=jnp.int32)).reshape(-1)
        key_owner = lineage[:, 0].reshape(micro, F, C, rows)
        key_owner = axis_relative(axis_relative(key_owner, 1, f), 2, c).reshape(micro, slots)
        first_row = (f * C + c) * rows
        query_lin = lax.dynamic_slice_in_dim(lineage, first_row, rows, 2)
        query_index = first_row + jnp.arange(rows, dtype=jnp.int32)
        owner = key_owner[:, :, None]
        visible = (
            ((owner == query_lin[:, 0, None, :]) & (key_index[None, :, None] <= query_index))
            | (owner == query_lin[:, 1, None, :])
            | (owner == query_lin[:, 2, None, :])
        )
        mask = jnp.where(visible, 0.0, NEG_FILL).astype(bf16)
        counts = jnp.sum(visible.astype(f32).reshape(micro, slots // KEY_STEP, KEY_STEP, rows), 2)
        positions = (jnp.sum(counts, 1) - 1.0).reshape(micro * rows)
        seen = (jnp.max(counts, -1) > 0).astype(jnp.int32).reshape(-1)
        frequency = ROPE_BASE ** (-jnp.arange(HEAD // 2, dtype=f32) / (HEAD // 2))
        angles = positions[:, None] * frequency[None, :]
        cosine, sine = jnp.cos(angles), jnp.sin(angles)
        cosine = jnp.concatenate([cosine, cosine], 1)
        sine = jnp.concatenate([-sine, sine], 1)

        hold = lax.optimization_barrier
        far = C // 2
        in_first = gather_first_halves(in_own, "fsdp", F)
        in_first, mask, cosine, sine, seen, x = hold((in_first, mask, cosine, sine, seen, x))
        in_pieces = gather_rest(in_first, "fsdp", F)
        in_pieces, (out_own, cx_mine, expert_own) = held_pieces(
            in_pieces, (w_output.T, cx_mine, expert_own)
        )
        out_there = exchange_direct([out_own] * F, "fsdp", F)
        a, q, kv_own, in_all, router, gains = project_in(
            x.reshape(micro * rows, width), cosine, sine, in_pieces, micro, rows, experts
        )
        kv_ctx = jnp.concatenate(exchange_direct([kv_own] * C, "ctx", C), 1)
        kv_ctx, out_there, cx_mine = hold((kv_ctx, out_there, cx_mine))
        out_pieces = [(array, j * depth) for j, array in enumerate(out_there)]
        kv = exchange_direct([kv_ctx] * F, "fsdp", F)
        cx_there = [
            cx_mine if k == 0 else None if k == far else swap(cx_mine, "ctx", C, k)
            for k in range(C)
        ]
        cx_far, kv, cx_there, expert_own = hold((cx_mine, kv, cx_there, expert_own))
        kv = [(array, j * C * rows) for j, array in enumerate(kv)]
        expert_first = gather_first(expert_own, "fsdp", F)
        cx_there[far] = swap(cx_far, "ctx", C, far)
        branch, o, lse, wo_all = attend(seen, q, mask, kv, out_pieces)
        cx_other = [core(block) if k != far else None for k, block in enumerate(cx_there)]
        middle, b = second_norm(place, x, branch, core(pick(branch, 1 - t)), gains)
        b, middle, cx_there, cx_other = hold((b, middle, cx_there, cx_other))

        there = exchange_direct([b] * C, "ctx", C)
        expert_pieces = gather_rest(expert_first, "fsdp", F, 2)
        expert_there = [block for block in expert_first if block is not None]
        there, cx_there[far] = after((there, cx_there[far]), *expert_there)
        cx_other[far] = core(cx_there[far])
        cx_both = cx_there + cx_other
        b_both = there + [core(block) for block in there]
        part = rows // SLICES

        def to_sums(own, other):
            got = core(other)
            return [
                add_low(own[k * part : (k + 1) * part], got[k * part : (k + 1) * part])
                for k in range(C)
            ]

        outs, back_sums, sides = [], [], []
        sums = None
        for n in range(SLICES):
            out_mine, out_other, back_mine, back_other, *side = experts_rows(
                place,
                b_both,
                [n * part] * (2 * C),
                part,
                cx_both,
                after(router, *sums) if sums else router,
                expert_pieces,
                experts,
            )
            outs.append((out_mine, out_other))
            sides.append(side)
            sums = to_sums(back_mine, back_other)
            back_sums.append(exchange_direct(sums, "ctx", C))
        b_at = [n * part for n in range(SLICES) for _ in b_both]

        def first_round(pieces):
            return [scatter_first(pieces[2 * n + 1], "fsdp", F, n == 0) for n in range(2)]

        def other_rounds(pieces, got):
            return [scatter_rest(pieces[2 * n], got[n], "fsdp", F, n == 0) for n in range(2)]

        sides, _, outs = hold((sides, sums, outs))
        grads = experts_grads(b_both, cx_both, b_at, part, sides, local_experts, F)
        near = [k for k in range(C) if k != far]
        grads, back_near = hold((grads, [back_sums[0][k] for k in near]))
        for k, block in zip(near, back_near):
            back_sums[0][k] = block
        grads_got = first_round(grads)
        out_sums = [
            jnp.concatenate(pieces, 0) for pieces in zip(*[to_sums(*pair) for pair in outs])
        ]
        back_sums, out_sums = hold((back_sums, out_sums))
        out_far = out_sums[far]
        for k in range(1, C):
            if k != far:
                out_sums[k] = swap(out_sums[k], "ctx", C, k)
        dmiddle, go, dl, dgain_two = second_norm_back(
            back_sums, middle, b, cx_mine, gains, router, experts
        )
        go_all, dq, *dkv = attend_back(
            place, seen, go, core(go), q, o, lse, mask, cosine, sine, wo_all, kv, F
        )
        go_all, dq, dkv, out_sums, out_far, grads_got = hold(
            (go_all, dq, dkv, out_sums, out_far, grads_got)
        )
        grad_own = jnp.stack(other_rounds(grads, grads_got))
        out_sums[far] = swap(out_far, "ctx", C, far)
        dkv, grad_own, out_sums = hold((dkv, grad_own, out_sums))
        go_flat, o_flat = go_all.reshape(micro * rows, width), o.reshape(micro * rows, -1)

        dkv = exchange_direct(dkv, "fsdp", F)
        total = dkv[0].astype(f32)
        for piece in dkv[1:]:
            total = total + piece.astype(f32)
        total = total.astype(bf16).reshape(micro, C, rows, 2 * HEAD)
        dkv = exchange_direct([total[:, k] for k in range(C)], "ctx", C)
        gathered = lax.all_gather(grad_own, "ctx", axis=0)
        dkv, da = project_back(dkv, dq, cosine, sine, in_all)
        input_grad, dgain_one = first_norm_back(
            place, da, core(pick(da, 1 - t)), x, gains, dmiddle
        )
        attn_grads = attention_grads(
            a, go_flat, dq, dkv, o_flat, b, dl, dgain_one, dgain_two, experts, F
        )
        attn_got = first_round(attn_grads)
        pieces = other_rounds(attn_grads, attn_got)
        step = depth // C
        pieces = jnp.concatenate(pieces, 1)
        got = exchange_direct(
            [lax.dynamic_slice_in_dim(pieces, (c ^ k) * step, step, 0) for k in range(C)], "ctx", C
        )
        wide = w_query.shape[1]
        total = got[0].astype(f32)
        for piece in got[1:]:
            total = total + piece.astype(f32)
        total = total.astype(bf16)
        tail = total[:, wide + 2 * HEAD + o_flat.shape[1] :]
        total = jnp.concatenate([total[:, : wide + 2 * HEAD + o_flat.shape[1]], add_low(tail, core(tail))], 1)
        got = exchange_direct([total] * C, "ctx", C)
        grad_gate, grad_up, grad_down = assemble(gathered)
        got, grad_gate, grad_up, grad_down = hold((got, grad_gate, grad_up, grad_down))
        grad_q, grad_k, grad_v, grad_out, grad_small = assemble_attention(
            place, got, wide, o_flat.shape[1]
        )
        result = sum((piece.astype(f32) for piece in out_sums), middle).astype(bf16)

        def whole(mine_value):
            other = core(mine_value)
            both = jnp.stack([pick((mine_value, other), t), pick((other, mine_value), t)])
            return lanes_relative(both, f, F)

        return (
            whole(result),
            whole(input_grad),
            grad_small[:, experts],
            grad_q,
            grad_k,
            grad_v,
            grad_out,
            grad_small[:, experts + 1],
            grad_small[:, :experts],
            grad_gate,
            grad_up,
            grad_down,
        )

    rows_of = P(None, ("fsdp", "ctx"), None)
    weights = (
        P("fsdp"),
        P("fsdp", "tp"),
        P("fsdp", "tp"),
        P("fsdp", "tp"),
        P("tp", "fsdp"),
        P("fsdp"),
        P("fsdp", None),
        P(None, "fsdp", "tp"),
        P(None, "fsdp", "tp"),
        P(None, "tp", "fsdp"),
    )
    return jax.shard_map(
        local,
        mesh=mesh,
        in_specs=(rows_of, *weights, P(), rows_of, rows_of),
        out_specs=(rows_of, rows_of, *weights),
        check_vma=False,
    )
```

```python
import jax
import jax.numpy as jnp
from jax import lax
from jax.experimental import pallas as pl
from jax.experimental.pallas import tpu as pltpu
from jax.sharding import PartitionSpec as P

HEAD = 128
LANES = 128
EPSILON = 1e-06
ROPE_BASE = 1000000.0
NEG_FILL = -1e30
KEY_STEP = 256
MOE_ROWS = 512
SLICES = 1
VMEM_BYTES = 60 * 2**20

f32 = jnp.float32
bf16 = jnp.bfloat16
EXACT = lax.Precision.HIGHEST
NN = (((1,), (0,)), ((), ()))
NT = (((1,), (1,)), ((), ()))
TN = (((0,), (0,)), ((), ()))


def mm(left, right, dims=NN, precision=None):
    return lax.dot_general(left, right, dims, precision=precision, preferred_element_type=f32)


def vmem(count):
    return [pl.BlockSpec(memory_space=pltpu.VMEM)] * count


def anywhere(count):
    return [pl.BlockSpec(memory_space=pl.ANY)] * count


def scalars():
    return [pl.BlockSpec(memory_space=pltpu.SMEM)]


def shape(dims, kind):
    return jax.ShapeDtypeStruct(dims, kind)


def cost(flops, moved):
    return pl.CostEstimate(flops=int(flops), bytes_accessed=int(moved), transcendentals=0)


def params():
    return pltpu.CompilerParams(vmem_limit_bytes=VMEM_BYTES)


def swap(value, axis, size, bit):
    return lax.ppermute(value, axis, [(i, i ^ bit) for i in range(size)])


def low_bit(number):
    return number & -number


def high_bit(number):
    return 1 << (number.bit_length() - 1)


def after(value, *earlier):
    return lax.optimization_barrier((value, *earlier))[0]


def gather_first(own, axis, size):
    return [
        own if j == 0 else swap(own, axis, size, j) if low_bit(j) == high_bit(j) else None
        for j in range(size)
    ]


def gather_first_halves(own, axis, size):
    rows = own.shape[0] // 2
    halves = (own[:rows], own[rows:])
    return [
        halves
        if j == 0
        else tuple(swap(half, axis, size, j) for half in halves)
        if low_bit(j) == high_bit(j)
        else None
        for j in range(size)
    ]


def gather_rest(got, axis, size, dim=0, ties=()):
    got = list(got)
    rows = 2 * got[0][0].shape[dim] if isinstance(got[0], tuple) else got[0].shape[dim]

    def half(j, top):
        if isinstance(got[j], tuple):
            return got[j][0 if top else 1]
        begin = 0 if top else rows // 2
        return after(lax.slice_in_dim(got[j], begin, begin + rows // 2, axis=dim), *ties)

    for j in range(1, size):
        low, high = low_bit(j), high_bit(j)
        if low != high:
            got[j] = (
                swap(half(j ^ high, True), axis, size, high),
                swap(half(j ^ low, False), axis, size, low),
            )
    return [
        (piece, j * rows + row)
        for j, block in enumerate(got)
        for piece, row in (
            ((block[0], 0), (block[1], rows // 2)) if isinstance(block, tuple) else ((block, 0),)
        )
    ]


def held_pieces(pieces, others):
    arrays, others = lax.optimization_barrier(([array for array, _ in pieces], others))
    return [(array, row) for array, (_, row) in zip(arrays, pieces)], others


def add_low(left, right):
    return (left.astype(f32) + right.astype(f32)).astype(bf16)


def scatter_order(size, high):
    bits = size.bit_length() - 1
    if high:
        return list(range(size))
    return [sum(((n >> k) & 1) << (bits - 1 - k) for k in range(bits)) for n in range(size)]


def scatter_bits(size, high):
    bits = [1 << k for k in range(size.bit_length() - 1)]
    return bits[::-1] if high else bits


def scatter_first(send, axis, size, high):
    return swap(send, axis, size, scatter_bits(size, high)[0])


def scatter_rest(keep, got, axis, size, high):
    for bit in scatter_bits(size, high)[1:]:
        count = keep.shape[0] // 2
        send = add_low(keep[count:], got[count:])
        keep, got = add_low(keep[:count], got[:count]), swap(send, axis, size, bit)
    return add_low(keep[0], got[0])


def exchange_direct(blocks, axis, size):
    return [blocks[0]] + [swap(blocks[j], axis, size, j) for j in range(1, size)]


def axis_relative(value, dim, index):
    count, bit, dims = value.shape[dim], 1, value.shape
    while bit < count:
        split = value.reshape(*dims[:dim], count // (2 * bit), 2, bit, *dims[dim + 1 :])
        value = jnp.where((index & bit) != 0, jnp.flip(split, dim + 1), split).reshape(dims)
        bit *= 2
    return value


def lanes_relative(value, index, count):
    width = value.shape[-1] // count
    return jnp.concatenate(
        [
            lax.dynamic_slice_in_dim(value, (index ^ j) * width, width, value.ndim - 1)
            for j in range(count)
        ],
        -1,
    )


def rotated(values, cosine, sine):
    return values * cosine + pltpu.roll(values, HEAD // 2, 1) * sine


def norm_scale(values):
    return lax.rsqrt(jnp.mean(values * values, -1, keepdims=True) + EPSILON)


def fetch(sources, targets, sems):
    copies = [
        pltpu.make_async_copy(source, target, sems.at[number])
        for number, (source, target) in enumerate(zip(sources, targets))
    ]
    for copy in copies:
        copy.start()
    return copies


def project_in(x, cosine, sine, pieces, micro, rows, experts):
    total, width = x.shape
    parts = len(pieces)
    columns = pieces[0][0].shape[1] - LANES
    heads = (columns - 2 * HEAD) // HEAD

    def body(x_ref, cos_ref, sin_ref, *rest):
        w_refs, (a_ref, q_ref, kv_ref, all_ref, small_ref, gains_ref, sems) = rest[:parts], rest[parts:]
        copies = fetch(
            w_refs,
            [all_ref.at[pl.ds(row, array.shape[0]), :] for array, row in pieces],
            sems,
        )
        values = x_ref[...].astype(f32)
        normal = values * norm_scale(values)
        for copy in copies:
            copy.wait()
        small = all_ref[:, columns:]
        small_ref[...] = small
        gains = small.astype(f32).T[experts : experts + 8, :]
        gains_ref[...] = gains
        a_ref[...] = (normal * gains[0:1, :]).astype(bf16)
        for m in range(micro):
            span = slice(m * rows, (m + 1) * rows)
            mixed = mm(a_ref[span, :], all_ref[:, :columns])
            cosine_m, sine_m = cos_ref[span, :], sin_ref[span, :]
            for h in range(heads):
                q_ref[m, h * rows : (h + 1) * rows, :] = rotated(
                    mixed[:, h * HEAD : (h + 1) * HEAD], cosine_m, sine_m
                ).astype(bf16)
            kv_ref[m, :, :HEAD] = rotated(
                mixed[:, heads * HEAD : (heads + 1) * HEAD], cosine_m, sine_m
            ).astype(bf16)
            kv_ref[m, :, HEAD:] = mixed[:, (heads + 1) * HEAD :].astype(bf16)

    return pl.pallas_call(
        body,
        name="project_in",
        out_shape=(
            shape((total, width), bf16),
            shape((micro, heads * rows, HEAD), bf16),
            shape((micro, rows, 2 * HEAD), bf16),
            shape((width, columns + LANES), bf16),
            shape((width, LANES), bf16),
            shape((8, width), f32),
        ),
        in_specs=vmem(3) + anywhere(parts),
        out_specs=tuple(vmem(6)),
        scratch_shapes=[pltpu.SemaphoreType.DMA((parts,))],
        compiler_params=params(),
        cost_estimate=cost(2 * total * width * columns, 4 * width * columns),
    )(x, cosine, sine, *[array for array, _ in pieces])


def attend(seen, q, mask, kv, weights):
    micro, stacked, _ = q.shape
    keys, rows = mask.shape[1], mask.shape[2]
    heads = stacked // rows
    blocks, parts = len(kv), len(weights)
    width = sum(array.shape[0] for array, _ in weights)
    steps = keys // KEY_STEP
    scale = HEAD ** (-0.5)

    def body(seen_ref, q_ref, mask_ref, *rest):
        kv_refs, w_refs = rest[:blocks], rest[blocks : blocks + parts]
        branch_ref, o_ref, lse_ref, wo_ref, kv_all, top, total, acc, kv_sems, w_sems = rest[
            blocks + parts :
        ]
        kv_copies = fetch(
            kv_refs, [kv_all.at[:, pl.ds(row, array.shape[1]), :] for array, row in kv], kv_sems
        )
        w_copies = fetch(
            w_refs, [wo_ref.at[pl.ds(row, array.shape[0]), :] for array, row in weights], w_sems
        )
        for copy in kv_copies:
            copy.wait()
        for m in range(micro):
            top[...] = jnp.full_like(top, NEG_FILL)
            total[...] = jnp.zeros_like(total)
            acc[...] = jnp.zeros_like(acc)
            queries = q_ref[m]

            def step(n, carry, m=m, queries=queries):
                @pl.when(seen_ref[m * steps + n] > 0)
                def _():
                    start = pl.multiple_of(n * KEY_STEP, KEY_STEP)
                    keys_n = kv_all[m, pl.ds(start, KEY_STEP), :HEAD]
                    values_n = kv_all[m, pl.ds(start, KEY_STEP), HEAD:]
                    bias = mask_ref[m, pl.ds(start, KEY_STEP), :].astype(f32)
                    scores = mm(keys_n, queries, NT) * scale + jnp.concatenate([bias] * heads, 1)
                    peak = jnp.maximum(top[...], jnp.max(scores, 0, keepdims=True))
                    rescale = jnp.exp(top[...] - peak)
                    weights_n = jnp.exp(scores - peak)
                    total[...] = total[...] * rescale + jnp.sum(weights_n, 0, keepdims=True)
                    acc[...] = acc[...] * rescale + mm(values_n, weights_n.astype(bf16), TN)
                    top[...] = peak

                return carry

            lax.fori_loop(0, steps, step, 0)
            lse_ref[m] = top[...] + jnp.log(total[...])
            mixed = acc[...] / total[...]
            for h in range(heads):
                o_ref[m, :, h * HEAD : (h + 1) * HEAD] = mixed[
                    :, h * rows : (h + 1) * rows
                ].T.astype(bf16)
        for copy in w_copies:
            copy.wait()
        for m in range(micro):
            branch_ref[m] = mm(o_ref[m], wo_ref[...], NT).astype(bf16)

    return pl.pallas_call(
        body,
        name="attend",
        out_shape=(
            shape((micro, rows, width), bf16),
            shape((micro, rows, heads * HEAD), bf16),
            shape((micro, 1, stacked), f32),
            shape((width, heads * HEAD), bf16),
        ),
        in_specs=scalars() + vmem(2) + anywhere(blocks + parts),
        out_specs=tuple(vmem(4)),
        scratch_shapes=[
            pltpu.VMEM((micro, keys, 2 * HEAD), bf16),
            pltpu.VMEM((1, stacked), f32),
            pltpu.VMEM((1, stacked), f32),
            pltpu.VMEM((HEAD, stacked), f32),
            pltpu.SemaphoreType.DMA((blocks,)),
            pltpu.SemaphoreType.DMA((parts,)),
        ],
        compiler_params=params(),
        cost_estimate=cost(
            2 * micro * stacked * keys * HEAD * 2 + 2 * micro * rows * width * heads * HEAD,
            2 * micro * keys * 2 * HEAD + 2 * width * heads * HEAD * 2,
        ),
    )(seen, q, mask, *[array for array, _ in kv], *[array for array, _ in weights])


def second_norm(place, x, branch, other, gain):
    rows, width = other.shape

    def body(place_ref, x_ref, branch_ref, other_ref, gain_ref, middle_ref, b_ref):
        t = place_ref[2]
        middle = (
            x_ref[t].astype(f32) + branch_ref[t].astype(f32) + other_ref[...].astype(f32)
        )
        middle_ref[...] = middle
        b_ref[...] = (middle * norm_scale(middle) * gain_ref[1:2, :]).astype(bf16)

    return pl.pallas_call(
        body,
        name="second_norm",
        out_shape=(shape((rows, width), f32), shape((rows, width), bf16)),
        in_specs=scalars() + vmem(4),
        out_specs=tuple(vmem(2)),
        compiler_params=params(),
        cost_estimate=cost(10 * rows * width, 20 * rows * width),
    )(place, x, branch, other, gain)


def routing(b, router, experts):
    logits = mm(b, router)
    lane = lax.broadcasted_iota(jnp.int32, logits.shape, 1)
    logits = jnp.where(lane < experts, logits, NEG_FILL)
    powers = jnp.exp(logits - jnp.max(logits, -1, keepdims=True))
    return powers / jnp.sum(powers, -1, keepdims=True), lane


def experts_rows(place, b, at, block, cx, router, weights, experts):
    pieces, width = len(at), b[0].shape[1]
    total = pieces * block
    rows = min(MOE_ROWS, total)
    local, _, _, hidden = weights[0][0].shape
    wide = local * hidden
    w_count = len(weights)
    half_rows = total // 2
    k0 = 0.7978845608028654
    k1 = 0.044715

    def body(place_ref, router_ref, *rest):
        b_refs, cx_refs = rest[: len(b)], rest[len(b) : 2 * len(b)]
        w_refs, rest = rest[2 * len(b) : 2 * len(b) + w_count], rest[2 * len(b) + w_count :]
        out_refs, back_refs, side_refs = rest[:2], rest[2:4], rest[4:7]
        b_all, cx_all, w_all, out_low, back_low, sides, b_sems, cx_sems, w_sems, o_sems = rest[7:]
        scaled_ref, gate_ref, up_ref = (sides.at[n] for n in range(3))
        o_copies = []

        def send(source, target):
            copy = pltpu.make_async_copy(source, target, o_sems.at[len(o_copies)])
            copy.start()
            o_copies.append(copy)

        row_copies = fetch(
            [b_refs[n % len(b)].at[pl.ds(row, block), :] for n, row in enumerate(at)],
            [b_all.at[pl.ds(n * block, block), :] for n in range(pieces)],
            b_sems,
        )
        w_copies = fetch(
            [ref.at[e] for ref in w_refs for e in range(local)],
            [
                w_all.at[:, pl.ds(row, array.shape[2]), pl.ds(e * hidden, hidden)]
                for array, row in weights
                for e in range(local)
            ],
            w_sems,
        )
        row_copies += fetch(
            [cx_refs[n % len(b)].at[pl.ds(row, block), :] for n, row in enumerate(at)],
            [cx_all.at[pl.ds(n * block, block), :] for n in range(pieces)],
            cx_sems,
        )
        for copy in row_copies:
            copy.wait()
        lane = lax.broadcasted_iota(jnp.int32, (rows, LANES), 1)
        for start in range(0, total, rows):
            span = slice(start, start + rows)
            probs, _ = routing(b_all[span, :], router_ref[...], experts)
            gates = probs * cx_all[span, width:].astype(f32)
            mine = [lane == place_ref[1] * local + e for e in range(local)]
            gate = jnp.concatenate(
                [
                    jnp.broadcast_to(
                        jnp.sum(jnp.where(mine[e], gates, 0.0), -1, keepdims=True), (rows, hidden)
                    )
                    for e in range(local)
                ],
                1,
            )
            if start == 0:
                for copy in w_copies:
                    copy.wait()
            b_rows = b_all[span, :]
            z = mm(b_rows, w_all[0])
            up = mm(b_rows, w_all[1])
            down_back = mm(cx_all[span, :width], w_all[2])
            square = z * z
            bend = jnp.tanh(k0 * z * (1.0 + k1 * square))
            half = 0.5 * (1.0 + bend)
            active = z * half
            slope = half + 0.5 * z * (1.0 - bend * bend) * (k0 * (1.0 + 3.0 * k1 * square))
            hidden_rows = active * up
            hidden_back = gate * down_back
            scaled_ref[span, :] = (gate * hidden_rows).astype(bf16)
            gate_ref[span, :] = (hidden_back * up * slope).astype(bf16)
            up_ref[span, :] = (hidden_back * active).astype(bf16)
            product = hidden_rows * down_back
            share = jnp.zeros((rows, LANES), f32)
            for e in range(local):
                share += jnp.where(
                    mine[e],
                    jnp.sum(product[:, e * hidden : (e + 1) * hidden], -1, keepdims=True),
                    0.0,
                )
            for n in range(3):
                send(sides.at[n, pl.ds(start, rows), :], side_refs[n].at[pl.ds(start, rows), :])
            out_low[span, :] = mm(scaled_ref[span, :], w_all[2], NT).astype(bf16)
            back_low[span, :width] = (
                mm(gate_ref[span, :], w_all[0], NT) + mm(up_ref[span, :], w_all[1], NT)
            ).astype(bf16)
            back_low[span, width:] = share.astype(bf16)
            for n in range(2):
                low, high = max(start, n * half_rows), min(start + rows, (n + 1) * half_rows)
                if low < high:
                    to = pl.ds(low - n * half_rows, high - low)
                    send(out_low.at[pl.ds(low, high - low), :], out_refs[n].at[to, :])
                    send(back_low.at[pl.ds(low, high - low), :], back_refs[n].at[to, :])
        for copy in o_copies:
            copy.wait()

    return pl.pallas_call(
        body,
        name="experts_rows",
        out_shape=(
            *[shape((half_rows, width), bf16)] * 2,
            *[shape((half_rows, width + LANES), bf16)] * 2,
            *[shape((total, wide), bf16)] * 3,
        ),
        in_specs=scalars() + vmem(1) + anywhere(2 * len(b) + w_count),
        out_specs=tuple(anywhere(7)),
        scratch_shapes=[
            pltpu.VMEM((total, width), bf16),
            pltpu.VMEM((total, width + LANES), bf16),
            pltpu.VMEM((3, width, wide), bf16),
            pltpu.VMEM((total, width), bf16),
            pltpu.VMEM((total, width + LANES), bf16),
            pltpu.VMEM((3, total, wide), bf16),
            pltpu.SemaphoreType.DMA((pieces,)),
            pltpu.SemaphoreType.DMA((pieces,)),
            pltpu.SemaphoreType.DMA((local * w_count,)),
            pltpu.SemaphoreType.DMA((7 * total // rows,)),
        ],
        compiler_params=params(),
        cost_estimate=cost(12 * total * width * wide, 2 * (4 * total * width + 3 * width * wide)),
    )(place, router, *b, *cx, *[array for array, _ in weights])


def experts_grads(b, cx, at, block, sides, local, parts):
    pieces, width = len(at), b[0].shape[1]
    total = pieces * block
    calls = len(sides)
    each = total // calls
    wide = sides[0][0].shape[1]
    hidden, depth, half = wide // local, width // parts, parts // 2
    fine = depth // 2
    orders = [scatter_order(parts, n == 0) for n in range(2)]

    def body(*refs):
        b_refs, cx_refs, side_refs = refs[: len(b)], refs[len(b) : 2 * len(b)], refs[2 * len(b) :]
        side_refs, rest = side_refs[: 3 * calls], side_refs[3 * calls :]
        grad_refs = rest[:4]
        b_all, c_all, side_all, turned, stage, b_sems, c_sems, s_sems, g_sems = rest[4:]
        b_copies = fetch(
            [b_refs[n % len(b)].at[pl.ds(row, block), :] for n, row in enumerate(at)],
            [b_all.at[pl.ds(n * block, block), :] for n in range(pieces)],
            b_sems,
        )
        s_copies = fetch(
            side_refs,
            [
                side_all.at[n, pl.ds(call * each, each), :]
                for call in range(calls)
                for n in range(3)
            ],
            s_sems,
        )
        c_copies = fetch(
            [
                cx_refs[n % len(b)].at[pl.ds(row, block), pl.ds(0, width)]
                for n, row in enumerate(at)
            ],
            [c_all.at[pl.ds(n * block, block), :] for n in range(pieces)],
            c_sems,
        )
        for copy in b_copies + s_copies:
            copy.wait()
        g_copies = []
        for n, side in ((0, 1), (1, 2), (2, 0)):
            if n == 0:
                turned[...] = b_all[...].T
            if n == 2:
                for copy in c_copies:
                    copy.wait()
                turned[...] = c_all[...].T
            for j in range(parts):
                span = slice(j * depth, (j + 1) * depth)
                stage[n, span, :] = mm(turned[span, :], side_all[side]).astype(bf16)
                for e in range(local):
                    for way in range(2):
                        to = orders[way].index(j)
                        copy = pltpu.make_async_copy(
                            stage.at[
                                n, pl.ds(j * depth + way * fine, fine), pl.ds(e * hidden, hidden)
                            ],
                            grad_refs[2 * way + to // half].at[to % half, e, n],
                            g_sems.at[len(g_copies)],
                        )
                        copy.start()
                        g_copies.append(copy)
        for copy in g_copies:
            copy.wait()

    return pl.pallas_call(
        body,
        name="experts_grads",
        out_shape=tuple([shape((half, local, 3, fine, hidden), bf16)] * 4),
        in_specs=anywhere(2 * len(b) + 3 * calls),
        out_specs=tuple(anywhere(4)),
        scratch_shapes=[
            pltpu.VMEM((total, width), bf16),
            pltpu.VMEM((total, width), bf16),
            pltpu.VMEM((3, total, wide), bf16),
            pltpu.VMEM((width, total), bf16),
            pltpu.VMEM((3, width, wide), bf16),
            pltpu.SemaphoreType.DMA((pieces,)),
            pltpu.SemaphoreType.DMA((pieces,)),
            pltpu.SemaphoreType.DMA((3 * calls,)),
            pltpu.SemaphoreType.DMA((3 * parts * local * 2,)),
        ],
        compiler_params=params(),
        cost_estimate=cost(
            6 * total * width * wide, 2 * (2 * total * width + 3 * total * wide + 3 * width * wide)
        ),
    )(*b, *cx, *[array for side in sides for array in side])


def second_norm_back(sums, middle, b, cx, gain, router, experts):
    rows, width = middle.shape
    slices, count = len(sums), len(sums[0])
    part = rows // slices

    def body(*refs):
        sum_refs, refs = refs[: slices * count], refs[slices * count :]
        middle_ref, b_ref, cx_ref, gain_ref, router_ref, dmiddle_ref, go_ref, dl_ref, dgain_ref = refs
        weights = router_ref[...]
        for n in range(slices):
            span = slice(n * part, (n + 1) * part)
            total = sum_refs[n * count][...].astype(f32)
            for ref in sum_refs[n * count + 1 : (n + 1) * count]:
                total += ref[...].astype(f32)
            b_rows = b_ref[span, :]
            share = total[:, width:] * cx_ref[span, width:].astype(f32)
            probs, _ = routing(b_rows, weights, experts)
            dl = probs * (share - jnp.sum(probs * share, -1, keepdims=True))
            dl_high = dl.astype(bf16)
            dl_low = (dl - dl_high.astype(f32)).astype(bf16)
            db = total[:, :width] + mm(dl_high, weights, NT) + mm(dl_low, weights, NT)
            values = middle_ref[span, :]
            scale = norm_scale(values)
            normal = values * scale
            dn = db * gain_ref[1:2, :]
            dmiddle = cx_ref[span, :width].astype(f32) + scale * (
                dn - normal * jnp.mean(dn * normal, -1, keepdims=True)
            )
            dmiddle_ref[span, :] = dmiddle
            go_ref[span, :] = dmiddle.astype(bf16)
            dl_ref[span, :] = dl_high
            dgain_ref[span, :] = (db * normal).astype(bf16)

    return pl.pallas_call(
        body,
        name="second_norm_back",
        out_shape=(
            shape((rows, width), f32),
            shape((rows, width), bf16),
            shape((rows, LANES), bf16),
            shape((rows, width), bf16),
        ),
        in_specs=vmem(slices * count + 5),
        out_specs=tuple(vmem(4)),
        compiler_params=params(),
        cost_estimate=cost(2 * 20 * rows * width * LANES, 24 * rows * width),
    )(*[part for one in sums for part in one], middle, b, cx, gain, router)


def attend_back(place, seen, go_own, go_other, q, o, lse, mask, cosine, sine, wo, kv, groups):
    micro, stacked, _ = q.shape
    keys, rows = mask.shape[1], mask.shape[2]
    heads = stacked // rows
    blocks = len(kv)
    per_group = keys // groups
    width = wo.shape[0]
    steps = keys // KEY_STEP
    scale = HEAD ** (-0.5)

    def body(place_ref, seen_ref, own_ref, other_ref, q_ref, o_ref, lse_ref, mask_ref, cos_ref, sin_ref, wo_ref, *rest):
        kv_refs = rest[:blocks]
        go_ref, dq_ref = rest[blocks : blocks + 2]
        dkv_refs = rest[blocks + 2 : blocks + groups + 2]
        kv_all, dkv_all, acc, do_all, kv_sems, d_sems = rest[blocks + groups + 2 :]
        kv_copies = fetch(
            kv_refs, [kv_all.at[:, pl.ds(row, array.shape[1]), :] for array, row in kv], kv_sems
        )
        t = place_ref[2]
        go_ref[t] = own_ref[...]
        go_ref[1 - t] = other_ref[...]
        for copy in kv_copies:
            copy.wait()
        for m in range(micro):
            do = mm(go_ref[m], wo_ref[...]).astype(bf16)
            pieces = []
            for h in range(heads):
                do_h = do[:, h * HEAD : (h + 1) * HEAD]
                do_all[h * rows : (h + 1) * rows, :] = do_h
                product = do_h.astype(f32) * o_ref[m, :, h * HEAD : (h + 1) * HEAD].astype(f32)
                pieces.append(jnp.sum(product.T, 0, keepdims=True))
            delta = jnp.concatenate(pieces, 1)
            acc[...] = jnp.zeros_like(acc)
            queries, outs, total = q_ref[m], do_all[...], lse_ref[m]

            def step(n, carry, m=m, queries=queries, outs=outs, total=total, delta=delta):
                start = pl.multiple_of(n * KEY_STEP, KEY_STEP)
                span = pl.ds(start, KEY_STEP)

                @pl.when(seen_ref[m * steps + n] > 0)
                def _():
                    keys_n = kv_all[m, span, :HEAD]
                    values_n = kv_all[m, span, HEAD:]
                    bias = mask_ref[m, span, :].astype(f32)
                    scores = mm(keys_n, queries, NT) * scale + jnp.concatenate([bias] * heads, 1)
                    probs = jnp.exp(scores - total)
                    ds = (probs * (mm(values_n, outs, NT) - delta)).astype(bf16)
                    acc[...] += mm(keys_n, ds, TN)
                    dkv_all[m, span, :HEAD] = (mm(ds, queries) * scale).astype(bf16)
                    dkv_all[m, span, HEAD:] = mm(probs.astype(bf16), outs).astype(bf16)

                @pl.when(seen_ref[m * steps + n] == 0)
                def _():
                    dkv_all[m, span, :] = jnp.zeros((KEY_STEP, 2 * HEAD), bf16)

                return carry

            lax.fori_loop(0, steps, step, 0)
            for h in range(heads):
                back = acc[:, h * rows : (h + 1) * rows].T * scale
                part = slice(m * rows, (m + 1) * rows)
                dq_ref[part, h * HEAD : (h + 1) * HEAD] = rotated(
                    back, cos_ref[part, :], -sin_ref[part, :]
                ).astype(bf16)
        d_copies = fetch(
            [dkv_all.at[:, pl.ds(j * per_group, per_group), :] for j in range(groups)], dkv_refs, d_sems
        )
        for copy in d_copies:
            copy.wait()

    return pl.pallas_call(
        body,
        name="attend_back",
        out_shape=(
            shape((micro, rows, width), bf16),
            shape((micro * rows, heads * HEAD), bf16),
            *[shape((micro, per_group, 2 * HEAD), bf16)] * groups,
        ),
        in_specs=scalars() * 2 + vmem(9) + anywhere(blocks),
        out_specs=(*vmem(2), *anywhere(groups)),
        scratch_shapes=[
            pltpu.VMEM((micro, keys, 2 * HEAD), bf16),
            pltpu.VMEM((micro, keys, 2 * HEAD), bf16),
            pltpu.VMEM((HEAD, stacked), f32),
            pltpu.VMEM((stacked, HEAD), bf16),
            pltpu.SemaphoreType.DMA((blocks,)),
            pltpu.SemaphoreType.DMA((groups,)),
        ],
        compiler_params=params(),
        cost_estimate=cost(
            2 * micro * stacked * keys * HEAD * 5,
            2 * micro * keys * 4 * HEAD + 2 * width * heads * HEAD,
        ),
    )(place, seen, go_own, go_other, q, o, lse, mask, cosine, sine, wo, *[array for array, _ in kv])


def project_back(dkv, dq, cosine, sine, w):
    count = len(dkv)
    micro, rows, _ = dkv[0].shape
    width, columns = w.shape
    columns -= LANES
    wide = columns - 2 * HEAD

    def body(*refs):
        dq_ref, cos_ref, sin_ref, w_ref, dkv_ref, da_ref = refs[count:]
        for m in range(micro):
            part = slice(m * rows, (m + 1) * rows)
            total = refs[0][m].astype(f32)
            for ref in refs[1:count]:
                total += ref[m].astype(f32)
            dkv_ref[part, :HEAD] = rotated(
                total[:, :HEAD], cos_ref[part, :], -sin_ref[part, :]
            ).astype(bf16)
            dkv_ref[part, HEAD:] = total[:, HEAD:].astype(bf16)
            da_ref[m] = (
                mm(dq_ref[part, :], w_ref[:, :wide], NT) + mm(dkv_ref[part, :], w_ref[:, wide:columns], NT)
            ).astype(bf16)

    return pl.pallas_call(
        body,
        name="project_back",
        out_shape=(shape((micro * rows, 2 * HEAD), bf16), shape((micro, rows, width), bf16)),
        in_specs=vmem(count + 4),
        out_specs=tuple(vmem(2)),
        compiler_params=params(),
        cost_estimate=cost(2 * micro * rows * width * columns, 2 * width * columns),
    )(*dkv, dq, cosine, sine, w)


def first_norm_back(place, da, other, x, gain, dmiddle):
    rows, width = dmiddle.shape

    def body(place_ref, da_ref, other_ref, x_ref, gain_ref, dmiddle_ref, ig_ref, dgain_ref):
        t = place_ref[2]
        total = da_ref[t].astype(f32) + other_ref[...].astype(f32)
        values = x_ref[t].astype(f32)
        scale = norm_scale(values)
        normal = values * scale
        dn = total * gain_ref[0:1, :]
        ig_ref[...] = dmiddle_ref[...] + scale * (
            dn - normal * jnp.mean(dn * normal, -1, keepdims=True)
        )
        dgain_ref[...] = (total * normal).astype(bf16)

    return pl.pallas_call(
        body,
        name="first_norm_back",
        out_shape=(shape((rows, width), f32), shape((rows, width), bf16)),
        in_specs=scalars() + vmem(5),
        out_specs=tuple(vmem(2)),
        compiler_params=params(),
        cost_estimate=cost(2 * 6 * rows * width * LANES, 20 * rows * width),
    )(place, da, other, x, gain, dmiddle)


def assemble(gathered):
    count, _, local, _, fine, hidden = gathered.shape
    depth = 2 * fine

    def body(in_ref, gate_ref, up_ref, down_ref):
        for way in range(2):
            span = slice(way * fine, (way + 1) * fine)
            gate_ref[0, span, :] = in_ref[0, way, 0, 0].astype(f32)
            up_ref[0, span, :] = in_ref[0, way, 0, 1].astype(f32)
            down_ref[0, :, span] = in_ref[0, way, 0, 2].astype(f32).T

    at = lambda j, e: (j * local + e, 0, 0)
    return pl.pallas_call(
        body,
        name="assemble",
        grid=(count, local),
        in_specs=[
            pl.BlockSpec((1, 2, 1, 3, fine, hidden), lambda j, e: (j, 0, e, 0, 0, 0))
        ],
        out_specs=(
            pl.BlockSpec((1, depth, hidden), at),
            pl.BlockSpec((1, depth, hidden), at),
            pl.BlockSpec((1, hidden, depth), at),
        ),
        out_shape=(
            *[shape((count * local, depth, hidden), f32)] * 2,
            shape((count * local, hidden, depth), f32),
        ),
        compiler_params=params(),
        cost_estimate=cost(count * local * depth * hidden * 3, count * local * depth * hidden * 18),
    )(gathered)


def assemble_attention(place, blocks, wide, out_wide):
    count = len(blocks)
    step, total = blocks[0].shape
    depth = count * step
    tail = total - wide - 2 * HEAD - out_wide

    def body(place_ref, *refs):
        q_ref, k_ref, v_ref, out_ref, small_ref, whole = refs[count:]
        for n in range(count):
            row = pl.multiple_of(lax.bitwise_xor(place_ref[1], n) * step, 8)
            whole[pl.ds(row, step), :] = refs[n][...].astype(f32)
        q_ref[...] = whole[:, :wide]
        k_ref[...] = whole[:, wide : wide + HEAD]
        v_ref[...] = whole[:, wide + HEAD : wide + 2 * HEAD]
        out_ref[...] = whole[:, wide + 2 * HEAD : wide + 2 * HEAD + out_wide].T
        small_ref[...] = whole[:, wide + 2 * HEAD + out_wide :]

    return pl.pallas_call(
        body,
        name="assemble_attention",
        out_shape=(
            shape((depth, wide), f32),
            shape((depth, HEAD), f32),
            shape((depth, HEAD), f32),
            shape((out_wide, depth), f32),
            shape((depth, tail), f32),
        ),
        in_specs=scalars() + vmem(count),
        out_specs=tuple(vmem(5)),
        scratch_shapes=[pltpu.VMEM((depth, total), f32)],
        compiler_params=params(),
        cost_estimate=cost(depth * total, 6 * depth * total),
    )(place, *blocks)


def attention_grads(a, go, dq, dkv, o, b, dl, dgain_one, dgain_two, experts, parts):
    rows, width = a.shape
    depth = width // parts
    half = parts // 2
    lanes = (dq.shape[1] + dkv.shape[1], o.shape[1] + LANES)

    def body(a_ref, go_ref, dq_ref, dkv_ref, o_ref, b_ref, dl_ref, one_ref, two_ref, *out_refs):
        def put(n, lane, total):
            for to, j in enumerate(scatter_order(parts, n == 0)):
                out_refs[2 * n + to // half][to % half, :, lane : lane + total.shape[1]] = total[
                    j * depth : (j + 1) * depth
                ].astype(bf16)

        turned = a_ref[...].T
        put(0, 0, mm(turned, dq_ref[...]))
        put(0, dq_ref.shape[1], mm(turned, dkv_ref[...]))
        put(1, 0, mm(go_ref[...].T, o_ref[...]))
        lane = lax.broadcasted_iota(jnp.int32, dl_ref.shape, 1)
        put(
            1,
            o_ref.shape[1],
            mm(b_ref[...].T, dl_ref[...])
            + mm(one_ref[...].T, (lane == experts).astype(bf16))
            + mm(two_ref[...].T, (lane == experts + 1).astype(bf16)),
        )

    return pl.pallas_call(
        body,
        name="attention_grads",
        out_shape=tuple(shape((half, depth, lanes[n // 2]), bf16) for n in range(4)),
        in_specs=vmem(9),
        out_specs=tuple(vmem(4)),
        compiler_params=params(),
        cost_estimate=cost(2 * rows * width * sum(lanes), 2 * width * sum(lanes)),
    )(a, go, dq, dkv, o, b, dl, dgain_one, dgain_two)


def solution(mesh):
    F, C, T = mesh.shape["fsdp"], mesh.shape["ctx"], mesh.shape["tp"]

    def local(
        tokens,
        gain_attn,
        w_query,
        w_key,
        w_value,
        w_output,
        gain_mlp,
        w_router,
        w_gate,
        w_up,
        w_down,
        lineage,
        expert_ids,
        cotangent,
    ):
        micro, rows, width = tokens.shape
        depth = width // F
        experts = w_router.shape[1]
        local_experts = experts // C
        slots = lineage.shape[2]
        f, c, t = lax.axis_index("fsdp"), lax.axis_index("ctx"), lax.axis_index("tp")
        place = jnp.stack([f, c, t]).astype(jnp.int32)

        def pick(pair, index):
            return jnp.where(index == 0, pair[0], pair[1])

        def core(value):
            return swap(value, "tp", T, 1)

        small = jnp.concatenate(
            [
                w_router,
                gain_attn[:, None],
                gain_mlp[:, None],
                jnp.zeros((depth, LANES - experts - 2), bf16),
            ],
            1,
        )
        in_own = jnp.concatenate([w_query, w_key, w_value, small], 1)

        def experts_of(index):
            mine = [
                lax.dynamic_slice_in_dim(w, index * local_experts, local_experts, 0)
                for w in (w_gate, w_up, w_down)
            ]
            return jnp.stack([mine[0], mine[1], jnp.swapaxes(mine[2], 1, 2)], 1)

        expert_own = experts_of(c)

        x = lanes_relative(tokens, f, F)
        c_mine = lanes_relative(pick(cotangent, t), f, F)
        ids_mine = pick(expert_ids, t)
        chosen = jnp.sum(
            (ids_mine[:, :, None] == jnp.arange(LANES, dtype=jnp.int32)[None, None, :]).astype(f32), 1
        ).astype(bf16)
        cx_mine = jnp.concatenate([c_mine, chosen], 1)

        f_order = f ^ jnp.arange(F, dtype=jnp.int32)
        c_order = c ^ jnp.arange(C, dtype=jnp.int32)
        block_order = (f_order[:, None] * C + c_order[None, :]).reshape(-1)
        key_index = (block_order[:, None] * rows + jnp.arange(rows, dtype=jnp.int32)).reshape(-1)
        key_owner = lineage[:, 0].reshape(micro, F, C, rows)
        key_owner = axis_relative(axis_relative(key_owner, 1, f), 2, c).reshape(micro, slots)
        first_row = (f * C + c) * rows
        query_lin = lax.dynamic_slice_in_dim(lineage, first_row, rows, 2)
        query_index = first_row + jnp.arange(rows, dtype=jnp.int32)
        owner = key_owner[:, :, None]
        visible = (
            ((owner == query_lin[:, 0, None, :]) & (key_index[None, :, None] <= query_index))
            | (owner == query_lin[:, 1, None, :])
            | (owner == query_lin[:, 2, None, :])
        )
        mask = jnp.where(visible, 0.0, NEG_FILL).astype(bf16)
        counts = jnp.sum(visible.astype(f32).reshape(micro, slots // KEY_STEP, KEY_STEP, rows), 2)
        positions = (jnp.sum(counts, 1) - 1.0).reshape(micro * rows)
        seen = (jnp.max(counts, -1) > 0).astype(jnp.int32).reshape(-1)
        frequency = ROPE_BASE ** (-jnp.arange(HEAD // 2, dtype=f32) / (HEAD // 2))
        angles = positions[:, None] * frequency[None, :]
        cosine, sine = jnp.cos(angles), jnp.sin(angles)
        cosine = jnp.concatenate([cosine, cosine], 1)
        sine = jnp.concatenate([-sine, sine], 1)

        hold = lax.optimization_barrier
        far = C // 2
        in_first = gather_first_halves(in_own, "fsdp", F)
        in_first, mask, cosine, sine, seen, x = hold((in_first, mask, cosine, sine, seen, x))
        in_pieces = gather_rest(in_first, "fsdp", F)
        in_pieces, (out_own, cx_mine, expert_own) = held_pieces(
            in_pieces, (w_output.T, cx_mine, expert_own)
        )
        out_there = exchange_direct([out_own] * F, "fsdp", F)
        a, q, kv_own, in_all, router, gains = project_in(
            x.reshape(micro * rows, width), cosine, sine, in_pieces, micro, rows, experts
        )
        kv_ctx = jnp.concatenate(exchange_direct([kv_own] * C, "ctx", C), 1)
        kv_ctx, out_there, cx_mine = hold((kv_ctx, out_there, cx_mine))
        out_pieces = [(array, j * depth) for j, array in enumerate(out_there)]
        kv = exchange_direct([kv_ctx] * F, "fsdp", F)
        cx_there = [
            cx_mine if k == 0 else None if k == far else swap(cx_mine, "ctx", C, k)
            for k in range(C)
        ]
        cx_far, kv, cx_there, expert_own = hold((cx_mine, kv, cx_there, expert_own))
        kv = [(array, j * C * rows) for j, array in enumerate(kv)]
        expert_first = gather_first(expert_own, "fsdp", F)
        cx_there[far] = swap(cx_far, "ctx", C, far)
        branch, o, lse, wo_all = attend(seen, q, mask, kv, out_pieces)
        cx_other = [core(block) if k != far else None for k, block in enumerate(cx_there)]
        middle, b = second_norm(place, x, branch, core(pick(branch, 1 - t)), gains)
        b, middle, cx_there, cx_other = hold((b, middle, cx_there, cx_other))

        there = exchange_direct([b] * C, "ctx", C)
        expert_pieces = gather_rest(expert_first, "fsdp", F, 2)
        expert_there = [block for block in expert_first if block is not None]
        there, cx_there[far] = after((there, cx_there[far]), *expert_there)
        cx_other[far] = core(cx_there[far])
        cx_both = cx_there + cx_other
        b_both = there + [core(block) for block in there]
        part = rows // SLICES

        def to_sums(own, other):
            got = core(other)
            return [
                add_low(own[k * part : (k + 1) * part], got[k * part : (k + 1) * part])
                for k in range(C)
            ]

        outs, back_sums, sides = [], [], []
        sums = None
        for n in range(SLICES):
            out_mine, out_other, back_mine, back_other, *side = experts_rows(
                place,
                b_both,
                [n * part] * (2 * C),
                part,
                cx_both,
                after(router, *sums) if sums else router,
                expert_pieces,
                experts,
            )
            outs.append((out_mine, out_other))
            sides.append(side)
            sums = to_sums(back_mine, back_other)
            back_sums.append(exchange_direct(sums, "ctx", C))
        b_at = [n * part for n in range(SLICES) for _ in b_both]

        def first_round(pieces):
            return [scatter_first(pieces[2 * n + 1], "fsdp", F, n == 0) for n in range(2)]

        def other_rounds(pieces, got):
            return [scatter_rest(pieces[2 * n], got[n], "fsdp", F, n == 0) for n in range(2)]

        sides, _, outs = hold((sides, sums, outs))
        grads = experts_grads(b_both, cx_both, b_at, part, sides, local_experts, F)
        near = list(range(C - 1))
        grads, back_near = hold((grads, [back_sums[0][k] for k in near]))
        for k, block in zip(near, back_near):
            back_sums[0][k] = block
        grads_got = first_round(grads)
        out_sums = [
            jnp.concatenate(pieces, 0) for pieces in zip(*[to_sums(*pair) for pair in outs])
        ]
        back_sums, out_sums = hold((back_sums, out_sums))
        out_far = out_sums[far]
        for k in range(1, C):
            if k != far:
                out_sums[k] = swap(out_sums[k], "ctx", C, k)
        dmiddle, go, dl, dgain_two = second_norm_back(
            back_sums, middle, b, cx_mine, gains, router, experts
        )
        go_all, dq, *dkv = attend_back(
            place, seen, go, core(go), q, o, lse, mask, cosine, sine, wo_all, kv, F
        )
        go_all, dq, dkv, out_sums, out_far, grads_got = hold(
            (go_all, dq, dkv, out_sums, out_far, grads_got)
        )
        grad_own = jnp.stack(other_rounds(grads, grads_got))
        out_sums[far] = swap(out_far, "ctx", C, far)
        dkv, grad_own, out_sums = hold((dkv, grad_own, out_sums))
        go_flat, o_flat = go_all.reshape(micro * rows, width), o.reshape(micro * rows, -1)

        dkv = exchange_direct(dkv, "fsdp", F)
        total = dkv[0].astype(f32)
        for piece in dkv[1:]:
            total = total + piece.astype(f32)
        total = total.astype(bf16).reshape(micro, C, rows, 2 * HEAD)
        dkv = exchange_direct([total[:, k] for k in range(C)], "ctx", C)
        gathered = lax.all_gather(grad_own, "ctx", axis=0)
        dkv, da = project_back(dkv, dq, cosine, sine, in_all)
        input_grad, dgain_one = first_norm_back(
            place, da, core(pick(da, 1 - t)), x, gains, dmiddle
        )
        attn_grads = attention_grads(
            a, go_flat, dq, dkv, o_flat, b, dl, dgain_one, dgain_two, experts, F
        )
        attn_got = first_round(attn_grads)
        pieces = other_rounds(attn_grads, attn_got)
        step = depth // C
        pieces = jnp.concatenate(pieces, 1)
        got = exchange_direct(
            [lax.dynamic_slice_in_dim(pieces, (c ^ k) * step, step, 0) for k in range(C)], "ctx", C
        )
        wide = w_query.shape[1]
        total = got[0].astype(f32)
        for piece in got[1:]:
            total = total + piece.astype(f32)
        total = total.astype(bf16)
        tail = total[:, wide + 2 * HEAD + o_flat.shape[1] :]
        total = jnp.concatenate([total[:, : wide + 2 * HEAD + o_flat.shape[1]], add_low(tail, core(tail))], 1)
        got = exchange_direct([total] * C, "ctx", C)
        grad_gate, grad_up, grad_down = assemble(gathered)
        got, grad_gate, grad_up, grad_down = hold((got, grad_gate, grad_up, grad_down))
        grad_q, grad_k, grad_v, grad_out, grad_small = assemble_attention(
            place, got, wide, o_flat.shape[1]
        )
        result = sum((piece.astype(f32) for piece in out_sums), middle).astype(bf16)

        def whole(mine_value):
            other = core(mine_value)
            both = jnp.stack([pick((mine_value, other), t), pick((other, mine_value), t)])
            return lanes_relative(both, f, F)

        return (
            whole(result),
            whole(input_grad),
            grad_small[:, experts],
            grad_q,
            grad_k,
            grad_v,
            grad_out,
            grad_small[:, experts + 1],
            grad_small[:, :experts],
            grad_gate,
            grad_up,
            grad_down,
        )

    rows_of = P(None, ("fsdp", "ctx"), None)
    weights = (
        P("fsdp"),
        P("fsdp", "tp"),
        P("fsdp", "tp"),
        P("fsdp", "tp"),
        P("tp", "fsdp"),
        P("fsdp"),
        P("fsdp", None),
        P(None, "fsdp", "tp"),
        P(None, "fsdp", "tp"),
        P(None, "tp", "fsdp"),
    )
    return jax.shard_map(
        local,
        mesh=mesh,
        in_specs=(rows_of, *weights, P(), rows_of, rows_of),
        out_specs=(rows_of, rows_of, *weights),
        check_vma=False,
    )
```
